128 devices in a mesh: ctx: 32 (over x, z, core), tp: 4 (over y).
Axes of the slice: x: 4, y: 4, z: 4, core: 2. Of those that a mesh axis runs over, the one named last changes fastest.
Arguments:
- residual: bfloat16 [8192, 8192], P('ctx', 'tp'), may hold values from -40 to 40
- query_in: bfloat16 [8192, 8192], P('ctx', 'tp'), may hold values from -6 to 6
- key_in: bfloat16 [8192, 8192], P('ctx', 'tp'), may hold values from -6 to 6
- value_in: bfloat16 [8192, 8192], P('ctx', 'tp'), may hold values from -6 to 6
- short_filter: float32 [3, 7, 8192], P(None, None, 'tp'), may hold values from -2 to 2
- residues: float32 [16, 8192], P(None, 'tp'), may hold values from -0.32 to 0.32
- decay_rate: float32 [16, 8192], P(None, 'tp'), may hold values from 2.4414063e-05 to 0.05
- skip_gain: float32 [8192], P('tp'), may hold values from 0.5 to 1.5
- norm_gain: float32 [8192], P('tp'), may hold values from 0.5 to 1.5
- cotangent: bfloat16 [8192, 8192], P('ctx', 'tp'), may hold values from -6 to 6
Outputs:
- normed: bfloat16 [8192, 8192], P('ctx', 'tp')
- grad_residual: bfloat16 [8192, 8192], P('ctx', 'tp')
- grad_query: bfloat16 [8192, 8192], P('ctx', 'tp')
- grad_key: bfloat16 [8192, 8192], P('ctx', 'tp')
- grad_value: bfloat16 [8192, 8192], P('ctx', 'tp')
- grad_short: float32 [3, 7, 8192], P(None, None, 'tp')
- grad_residues: float32 [16, 8192], P(None, 'tp')
- grad_rate: float32 [16, 8192], P(None, 'tp')
- grad_skip: float32 [8192], P('tp')
- grad_norm_gain: float32 [8192], P('tp')
The draws below stay inside these ranges and needn't reach their ends.
All inputs are finite; a program needn't handle non-finite values.
Results may differ from the reference program's by a relative error of at most 0.002.
Values may be sent and summed in bfloat16 or wider, within the bound.
A program may use at most 128 MiB of HBM per device.

```python
import math
import jax
import jax.numpy as jnp
from jax import lax

D = 8192
M = 16
KS = 7
TOK_DEV = 256
SEQ = 8192


def modal_pair(key):
    pick_key = jax.random.fold_in(key, 101)
    place_key = jax.random.fold_in(key, 202)
    sign_key = jax.random.fold_in(key, 303)
    slow_share = 0.5
    is_slow = jax.random.uniform(pick_key, (M, D)) < slow_share
    position = jax.random.uniform(place_key, (M, D))
    slow_low = math.log(0.2 / SEQ)
    slow_high = math.log(2.0 / SEQ)
    fast_high = math.log(0.05)
    log_rate = jnp.where(is_slow, slow_low + position * (slow_high - slow_low), slow_high + position * (fast_high - slow_high))
    rates = jnp.exp(log_rate)
    signs = jnp.clip(jax.random.normal(sign_key, (M, D)), -4.0, 4.0)
    return (rates, signs * jnp.sqrt(2.0 * rates) * 0.25)


def draw_decay_rate(key, part):
    return modal_pair(key)[0]


def draw_residues(key, part):
    return modal_pair(key)[1]


def draw_residual(key, part):
    noise_key = jax.random.fold_in(key, 404)
    row_key = jax.random.fold_in(key, 505)
    noise_values = jnp.clip(jax.random.normal(noise_key, (SEQ, D)), -4.0, 4.0)
    row_scale = jnp.exp(jax.random.uniform(row_key, (SEQ, 1)) * math.log(10.0))
    column_scale = jnp.exp(jnp.arange(D).astype(jnp.float32) / D * math.log(10.0))
    return (0.1 * noise_values * row_scale * column_scale[None, :]).astype(jnp.bfloat16)


def shard_levels(rng, dims, split, least, high):
    factor_of, own = 1.0, jax.random.fold_in(rng, 6)
    for axis_at, blocks in split:
        heights = jnp.exp(jax.random.uniform(jax.random.fold_in(own, axis_at), (blocks,), jnp.float32, least / len(split), high / len(split)))
        factor_of = factor_of * jnp.repeat(heights, dims[axis_at] // blocks).reshape([-1 if axis == axis_at else 1 for axis in range(len(dims))])
    return factor_of


def gaussian(own_key, dims, scale, bound, cuts=(), kind=jnp.bfloat16):
    values = scale * jax.random.normal(own_key, dims, jnp.float32)
    if cuts:
        values = values * shard_levels(own_key, dims, cuts, -0.22, 0.18)
    return jnp.clip(values, -bound, bound).astype(kind)


def setup_inputs(seed: int = 0) -> dict:
    streams_of = jax.random.split(jax.random.key(seed), 11)
    residual = draw_residual(jax.random.fold_in(streams_of[10], 71), 0)
    query_in = gaussian(streams_of[1], (SEQ, D), 1.0, 6.0, ((0, 32), (1, 4)))
    key_in = gaussian(streams_of[2], (SEQ, D), 1.0, 6.0, ((0, 32), (1, 4)))
    value_in = gaussian(streams_of[3], (SEQ, D), 1.0, 6.0, ((0, 32), (1, 4)))
    short_filter = gaussian(streams_of[4], (3, KS, D), KS ** -0.5, 2.0, ((2, 4),), jnp.float32)
    residues = draw_residues(jax.random.fold_in(streams_of[10], 71), 0)
    decay_rate = draw_decay_rate(jax.random.fold_in(streams_of[10], 71), 0)
    skip_gain = jnp.clip(0.5 + 1.0 * jax.random.uniform(streams_of[7], (D,), jnp.float32) ** shard_levels(streams_of[7], (D,), ((0, 4),), -0.2, 0.2), 0.5, 1.5)
    norm_gain = jnp.clip(1.0 + 0.1 * jax.random.normal(streams_of[8], (D,), jnp.float32), 0.5, 1.5)
    cotangent = gaussian(streams_of[9], (SEQ, D), 1.0, 6.0, ((0, 32), (1, 4)))
    return {"residual": residual, "query_in": query_in, "key_in": key_in, "value_in": value_in, "short_filter": short_filter, "residues": residues, "decay_rate": decay_rate, "skip_gain": skip_gain, "norm_gain": norm_gain, "cotangent": cotangent}


exact_mode = lax.Precision.HIGHEST

def make_tables(decay_rate, residues, block_len):
    lag_values = jnp.arange(block_len).astype(jnp.float32)
    powers = jnp.exp(-decay_rate[None, :, :] * lag_values[:, None, None])
    kernel = jnp.einsum('kmc,mc->kc', powers, residues, precision=exact_mode)
    offsets = jnp.arange(block_len)
    shifter = (offsets[:, None, None] - offsets[None, :, None] == offsets[None, None, :]).astype(jnp.float32)
    toeplitz = jnp.einsum('tsk,kc->tsc', shifter, kernel, precision=exact_mode)
    return (lag_values, powers, shifter, toeplitz)

def short_conv(extended, taps, row_count):
    tap_count = taps.shape[0]
    result = taps[0] * extended[tap_count - 1:tap_count - 1 + row_count]
    for offset in range(1, tap_count):
        result = result + taps[offset] * extended[tap_count - 1 - offset:tap_count - 1 - offset + row_count]
    return result

def conv_back(extended_grad, taps, row_count):
    tap_count = taps.shape[0]
    result = taps[0] * extended_grad[0:row_count]
    for offset in range(1, tap_count):
        result = result + taps[offset] * extended_grad[offset:offset + row_count]
    return result

def filter_grad(grad_feat, padded, tap_count, row_count):
    margin = tap_count - 1
    columns = [lax.optimization_barrier(jnp.sum(grad_feat * padded[margin - offset:margin - offset + row_count], axis=0)) for offset in range(tap_count)]
    return jnp.stack(columns)

def output_pass(u_blocks, state_x, state_p, decay_rate, residues, skip_gain, tables, track):
    lag_values, powers, shifter, toeplitz = tables
    block_len = powers.shape[0]
    ahead_pow = powers * jnp.exp(-decay_rate)[None]
    behind = powers[::-1]
    behind_lag = behind * lag_values[::-1][:, None, None]
    fading = jnp.exp(-decay_rate * block_len)

    def advance(running, u_block):
        state_x, state_p = running
        inside = jnp.einsum('tsc,sc->tc', toeplitz, u_block, precision=exact_mode)
        carried = jnp.einsum('tmc,mc->tc', ahead_pow, residues * state_x, precision=exact_mode)
        result = inside + carried + skip_gain * u_block
        gathered = jnp.einsum('smc,sc->mc', behind, u_block, precision=exact_mode)
        if track:
            weighted = jnp.einsum('smc,sc->mc', behind_lag, u_block, precision=exact_mode)
            state_p = fading * state_p - block_len * fading * state_x - weighted
        state_x = fading * state_x + gathered
        return ((state_x, state_p), result)
    (state_x, state_p), results = lax.scan(advance, (state_x, state_p), u_blocks)
    return (results, state_x, state_p)

def gradient_pass(u_blocks, dz_blocks, state_x, state_p, decay_rate, tables):
    lag_values, powers, shifter, toeplitz = tables
    block_len = powers.shape[0]
    ahead_pow = powers * jnp.exp(-decay_rate)[None]
    ahead_lag = ahead_pow * (lag_values + 1.0)[:, None, None]
    powers_lag = powers * lag_values[:, None, None]
    behind = powers[::-1]
    behind_lag = behind * lag_values[::-1][:, None, None]
    fading = jnp.exp(-decay_rate * block_len)

    def advance(running, pair):
        state_x, state_p, sum_res, sum_rate = running
        u_block, dz_block = pair
        products = dz_block[:, None, :] * u_block[None, :, :]
        lagged = jnp.einsum('tsk,tsc->kc', shifter, products, precision=exact_mode)
        nearby = jnp.einsum('tmc,tc->mc', ahead_pow, dz_block, precision=exact_mode)
        nearby_lag = jnp.einsum('tmc,tc->mc', ahead_lag, dz_block, precision=exact_mode)
        sum_res = sum_res + jnp.einsum('kc,kmc->mc', lagged, powers, precision=exact_mode) + nearby * state_x
        sum_rate = sum_rate - jnp.einsum('kc,kmc->mc', lagged, powers_lag, precision=exact_mode) - nearby_lag * state_x + nearby * state_p
        gathered = jnp.einsum('smc,sc->mc', behind, u_block, precision=exact_mode)
        weighted = jnp.einsum('smc,sc->mc', behind_lag, u_block, precision=exact_mode)
        state_p = fading * state_p - block_len * fading * state_x - weighted
        state_x = fading * state_x + gathered
        return ((state_x, state_p, sum_res, sum_rate), None)
    zero_sum = jnp.zeros_like(state_x)
    (state_x, state_p, sum_res, sum_rate), _ = lax.scan(advance, (state_x, state_p, zero_sum, zero_sum), (u_blocks, dz_blocks))
    return (sum_res, sum_rate)

def adjoint_pass(dz_blocks, adjoint, decay_rate, residues, tables):
    lag_values, powers, shifter, toeplitz = tables
    block_len = powers.shape[0]
    behind_next = powers[::-1] * jnp.exp(-decay_rate)[None]
    fading = jnp.exp(-decay_rate * block_len)

    def advance(adjoint, dz_block):
        inside = jnp.einsum('tsc,tc->sc', toeplitz, dz_block, precision=exact_mode)
        carried = jnp.einsum('smc,mc->sc', behind_next, residues * adjoint, precision=exact_mode)
        adjoint = jnp.einsum('tmc,tc->mc', powers, dz_block, precision=exact_mode) + fading * adjoint
        return (adjoint, inside + carried)
    adjoint, results = lax.scan(advance, adjoint, dz_blocks, reverse=True)
    return (results, adjoint)

def reference(residual, query_in, key_in, value_in, short_filter, residues, decay_rate, skip_gain, norm_gain, cotangent):
    block_len = min(32, TOK_DEV)
    margin = KS - 1
    streams = (query_in, key_in, value_in)
    padded = [jnp.concatenate([jnp.zeros((margin, D), jnp.float32), stream.astype(jnp.float32)], axis=0) for stream in streams]
    featured = [short_conv(padded[stream_id], short_filter[stream_id], SEQ) for stream_id in range(3)]
    mixed_uv = featured[1] * featured[2]
    tables = make_tables(decay_rate, residues, block_len)
    zero_state = jnp.zeros((M, D), jnp.float32)
    u_blocks = mixed_uv.reshape(SEQ // block_len, block_len, D)
    modal_blocks, _, _ = output_pass(u_blocks, zero_state, zero_state, decay_rate, residues, skip_gain, tables, False)
    modal = modal_blocks.reshape(SEQ, D)
    summed = residual.astype(jnp.float32) + featured[0] * modal
    inv_rms = lax.rsqrt(lax.optimization_barrier(jnp.sum(summed * summed, axis=1)) / D + 1e-05)
    normed = (summed * inv_rms[:, None] * norm_gain).astype(jnp.bfloat16)
    cot_values = cotangent.astype(jnp.float32)
    gain_term = cot_values * norm_gain
    inner_sum = lax.optimization_barrier(jnp.sum(gain_term * summed, axis=1))
    grad_sum = inv_rms[:, None] * gain_term - summed * (inv_rms ** 3 * inner_sum / D)[:, None]
    grad_modal = grad_sum * featured[0]
    grad_front = grad_sum * modal
    dz_blocks = grad_modal.reshape(SEQ // block_len, block_len, D)
    sum_res, sum_rate = gradient_pass(u_blocks, dz_blocks, zero_state, zero_state, decay_rate, tables)
    mixed_blocks, _ = adjoint_pass(dz_blocks, zero_state, decay_rate, residues, tables)
    grad_mixed = mixed_blocks.reshape(SEQ, D) + skip_gain * grad_modal
    grad_feats = (grad_front, grad_mixed * featured[2], grad_mixed * featured[1])
    zero_rows = jnp.zeros((margin, D), jnp.float32)
    grad_streams = [conv_back(jnp.concatenate([grad_feats[stream_id], zero_rows], axis=0), short_filter[stream_id], SEQ).astype(jnp.bfloat16) for stream_id in range(3)]
    grad_short = jnp.stack([filter_grad(grad_feats[stream_id], padded[stream_id], KS, SEQ) for stream_id in range(3)])
    grad_skip = lax.optimization_barrier(jnp.sum(grad_modal * mixed_uv, axis=0))
    grad_gain = lax.optimization_barrier(jnp.sum(cot_values * summed * inv_rms[:, None], axis=0))
    return (normed, grad_sum.astype(jnp.bfloat16), grad_streams[0], grad_streams[1], grad_streams[2], grad_short, sum_res, residues * sum_rate, grad_skip, grad_gain)
```

```python
import functools

import jax
import jax.numpy as jnp
from jax import lax
from jax.experimental import pallas as pl
from jax.experimental.pallas import tpu as pltpu
from jax.sharding import PartitionSpec as P

f32 = jnp.float32
bf16 = jnp.bfloat16
MESH = pl.DeviceIdType.MESH
B = 16
M = 16
KS = 7
HALO = KS - 1


def loop(count, step, start=0):
    def lap(i, carry):
        step(i)
        return carry

    lax.fori_loop(start, count, lap, 0)


def total(terms):
    terms = list(terms)
    while len(terms) > 1:
        terms = [
            terms[i] + terms[i + 1] if i + 1 < len(terms) else terms[i]
            for i in range(0, len(terms), 2)
        ]
    return terms[0]


def kernel(
    n, ntp, rows, width,
    res_h, q_h, k_h, v_h, sf_h, r_h, lam_h, skip_h, gain_h, cot_h,
    normed_o, gres_o, gq_o, gk_o, gv_o, short_o, gr_o, gl_o, gskip_o, ggain_o,
    nat, halo, sfv, rv, lv, skipv, gainv,
    QX, KX, VX, RS, CT, F0, F1, F2, U, Y, DZ, GS, G, GF0, GF1, GF2,
    AP, WP, KT, RT, SW, AT, XB, PB, AB,
    S1, R1, E1, X0, S2, R2, E2, A0,
    sums, tpr, INVT, CFT, RA, SA, CK, SG,
    T1, RR1, SUM1, AG1, T2, RR2, SUM2, AG2,
    shv, grv, glv,
    insem, outsem, ssem, rsem, hssem, hrsem,
):
    H = width // 1024
    nb = rows // B
    D = width * ntp
    me = lax.axis_index("ctx")
    mt = lax.axis_index("tp")
    tiles = H * M
    k1 = tiles // n
    k2 = 64 // n

    def peer(p):
        return (p, mt)

    ins = [
        (k_h, nat.at[2]), (v_h, nat.at[3]), (q_h, nat.at[1]), (res_h, nat.at[0]), (cot_h, nat.at[4]),
        (sf_h, sfv), (r_h, rv), (lam_h, lv), (skip_h, skipv), (gain_h, gainv),
    ]
    in_copies = [pltpu.make_async_copy(s, d, insem.at[i]) for i, (s, d) in enumerate(ins)]
    for copy in in_copies:
        copy.start()

    barrier = pltpu.get_barrier_semaphore()

    def greet(i):
        pl.semaphore_signal(
            barrier, inc=1, device_id=peer(lax.rem(me + i, n)), device_id_type=MESH
        )

    loop(n, greet, 1)
    for i in range(1, ntp):
        pl.semaphore_signal(
            barrier, inc=1, device_id=(me, lax.rem(mt + i, ntp)), device_id_type=MESH
        )
    pl.semaphore_wait(barrier, n - 1 + ntp - 1)

    def in_halo(i, src):
        return pltpu.make_async_remote_copy(
            src_ref=src.at[pl.ds(rows - 16, 16)], dst_ref=halo.at[i],
            send_sem=hssem.at[i], recv_sem=hrsem.at[i],
            device_id=peer(lax.rem(me + 1, n)), device_id_type=MESH,
        )

    halo_copies = [in_halo(0, q_h), in_halo(1, k_h), in_halo(2, v_h)]

    @pl.when(me < n - 1)
    def _():
        for copy in halo_copies:
            copy.start()

    for i in range(5, 10):
        in_copies[i].wait()
    for h in range(H):
        cols = pl.ds(h * 1024, 1024)
        lam = lv[:, cols].reshape(M, 8, 128)
        r = rv[:, cols].reshape(M, 8, 128)
        RT[h] = r
        AT[pl.ds(h * M, M)] = jnp.exp(lam * (-float(rows)))
        for i in range(3):
            SG[0:8, :] = jnp.zeros((8, 1024), f32)
            SG[0:KS, :] = sfv[i, :, cols]
            SW[i, h] = SG[0:8, :].reshape(8, 8, 128)

        def powers(k):
            p = jnp.exp(lam * (-k.astype(f32)))
            AP[h, k] = p
            WP[h, k] = p * k.astype(f32)
            KT[h, k] = jnp.sum(r * p, axis=0)

        loop(B + 1, powers)
        KT[h, 0] = KT[h, 0] + skipv[pl.ds(h * 8, 8), :]

    def to_tm(slot, dst, off):
        def step(i):
            v = nat[slot, pl.ds(pl.multiple_of(i * 16, 16), 16), :].astype(f32)
            dst[pl.ds(off + i * 16, 16)] = v.reshape(16, H, 8, 128)

        loop(rows // 16, step)

    in_copies[0].wait()
    to_tm(2, KX, 8)
    in_copies[1].wait()
    to_tm(3, VX, 8)
    in_copies[2].wait()
    to_tm(1, QX, 8)

    @pl.when(me > 0)
    def _():
        for copy in halo_copies:
            copy.wait_recv()

    @pl.when(me == 0)
    def _():
        halo[...] = jnp.zeros(halo.shape, bf16)

    for i, dst in enumerate((QX, KX, VX)):
        dst[pl.ds(0, 8)] = halo[i].astype(f32)[8:16].reshape(8, H, 8, 128)

    def window(src, b, h):
        return src[pl.ds(b * 8 + 2, 14), h]

    def fir(win, i, h):
        return total(SW[i, h, j][None] * win[HALO - j : HALO - j + 8] for j in range(KS))

    def feature(h):
        def step(b):
            at = pl.ds(b * 8, 8)
            f1 = fir(window(KX, b, h), 1, h)
            F1[at, h] = f1
            f2 = fir(window(VX, b, h), 2, h)
            F2[at, h] = f2
            U[at, h] = f1 * f2

        loop(rows // 8, step)

    loop(H, feature)

    def summary(h):
        a = AP[h, 1]

        def step(b, run):
            u = U[pl.ds(b * B, B), h]
            x = a * u[0][None] + u[1][None]
            for s in range(2, B):
                x = a * x + u[s][None]
            XB[h, b] = x
            return AP[h, B] * run + x

        S1[pl.ds(h * M, M)] = lax.fori_loop(0, nb, step, jnp.zeros((M, 8, 128), f32))

    loop(H, summary)

    def scatter(src, dst, size, at):
        def step(i):
            p = lax.rem(me + i, n)
            pltpu.make_async_remote_copy(
                src_ref=src.at[pl.ds(p * size, size)], dst_ref=dst.at[pl.ds(me * size, size)],
                send_sem=ssem.at[at], recv_sem=rsem.at[at],
                device_id=peer(p), device_id_type=MESH,
            ).start()

        loop(n, step, 1)
        mine = pl.ds(me * size, size)
        pltpu.make_async_copy(src.at[mine], dst.at[mine], rsem.at[at]).start()

    def spread(src, dst, size, at):
        mine = pl.ds(me * size, size)

        def step(i):
            p = lax.rem(me + i, n)
            pltpu.make_async_remote_copy(
                src_ref=src, dst_ref=dst.at[mine],
                send_sem=ssem.at[at], recv_sem=rsem.at[at],
                device_id=peer(p), device_id_type=MESH,
            ).start()

        loop(n, step, 1)
        pltpu.make_async_copy(src, dst.at[mine], rsem.at[at]).start()

    def arrived(dst, at):
        pltpu.make_async_copy(dst, dst, rsem.at[at]).wait()

    def sent(dst, size, at):
        part = dst.at[pl.ds(0, (n - 1) * size)]
        pltpu.make_async_copy(part, part, ssem.at[at]).wait()

    def scan(src, dst, backward):
        a = AT[pl.ds(me * k1, k1)]
        run = jnp.zeros((k1, 8, 128), f32)
        for i in range(n):
            d = n - 1 - i if backward else i
            at = pl.ds(d * k1, k1)
            dst[at] = run
            run = a * run + src[at]

    scatter(S1, R1, k1, 0)

    def feature_q(h):
        def step(b):
            F0[pl.ds(b * 8, 8), h] = fir(window(QX, b, h), 0, h)

        loop(rows // 8, step)

    loop(H, feature_q)

    def inside(h):
        def step(b):
            u = [U[b * B + t, h] for t in range(B)]
            kt = [KT[h, k] for k in range(B)]
            for t in range(B):
                Y[b * B + t, h] = total(kt[k] * u[t - k] for k in range(t + 1))

        loop(nb, step)

    loop(H, inside)
    arrived(R1, 0)
    scan(R1, E1, False)
    scatter(E1, X0, k1, 1)

    def weighted(h):
        def step(b):
            u = U[pl.ds(b * B, B), h]
            PB[h, b] = total_in_order([WP[h, B - s] * u[s][None] for s in range(B)])

        loop(nb, step)

    def total_in_order(terms):
        out = terms[0]
        for term in terms[1:]:
            out = out + term
        return out

    loop(H, weighted)
    in_copies[3].wait()
    to_tm(0, RS, 0)
    in_copies[4].wait()
    to_tm(4, CT, 0)
    arrived(X0, 1)

    def entry(h):
        def step(b, x):
            later = AP[h, B] * x + XB[h, b]
            XB[h, b] = x
            return later

        lax.fori_loop(0, nb, step, X0[pl.ds(h * M, M)])

    loop(H, entry)

    lane = lax.broadcasted_iota(jnp.int32, (B, 128), 1)
    sums[...] = jnp.zeros((B, 128), f32)

    def forward(b):
        squares = [None] * B
        inner = [None] * B
        for h in range(H):
            a = AP[h, 1]
            z = RT[h] * a * XB[h, b]
            gain = gainv[pl.ds(h * 8, 8), :]
            for i in range(B):
                t = b * B + i
                y = Y[t, h] + jnp.sum(z, axis=0)
                if i + 1 < B:
                    z = a * z
                Y[t, h] = y
                s = RS[t, h] + F0[t, h] * y
                RS[t, h] = s
                sq = s * s
                ip = CT[t, h] * gain * s
                squares[i] = sq if h == 0 else squares[i] + sq
                inner[i] = ip if h == 0 else inner[i] + ip

        def column(parts):
            return jnp.sum(jnp.stack(parts).reshape(B, 1024), axis=1, keepdims=True)

        now = jnp.where(lane == b, column(squares), sums[...])
        sums[...] = jnp.where(lane == nb + b, column(inner), now)

    loop(nb, forward)
    for i in range(1, ntp):
        p = lax.rem(mt + i, ntp)
        pltpu.make_async_remote_copy(
            src_ref=sums, dst_ref=tpr.at[mt], send_sem=ssem.at[8], recv_sem=rsem.at[8],
            device_id=(me, p), device_id_type=MESH,
        ).start()
    pltpu.make_async_copy(sums, tpr.at[mt], rsem.at[8]).start()
    pltpu.make_async_copy(tpr, tpr, rsem.at[8]).wait()
    tot = total(tpr[i] for i in range(ntp))
    inner_sum = pltpu.roll(tot, 128 - nb, 1)
    valid = lane < nb
    inv_all = lax.rsqrt(jnp.where(valid, tot, 1.0) / D + 1e-5)
    coef_all = inv_all * inv_all * inv_all * jnp.where(valid, inner_sum, 0.0) / D

    def spread_rows(b):
        at = pl.ds(b * B, B)
        for src, dst in ((inv_all, INVT), (coef_all, CFT)):
            col = jnp.sum(jnp.where(lane == b, src, 0.0), axis=1, keepdims=True)
            full = jnp.broadcast_to(col, (B, 128))
            dst[at] = jnp.broadcast_to(full[:, None, :], (B, 8, 128))

    loop(nb, spread_rows)

    def backward(h):
        a = AP[h, 1]

        def step(i, run):
            b = nb - 1 - i
            at = pl.ds(b * B, B)
            gain = gainv[pl.ds(h * 8, 8), :][None]
            gs = INVT[at] * (CT[at, h] * gain) - RS[at, h] * CFT[at]
            GS[at, h] = gs
            dz = gs * F0[at, h]
            DZ[at, h] = dz
            v = a * dz[B - 1][None] + dz[B - 2][None]
            for s in range(B - 3, -1, -1):
                v = a * v + dz[s][None]
            AB[h, b] = v
            return AP[h, B] * run + v

        S2[pl.ds(h * M, M)] = lax.fori_loop(0, nb, step, jnp.zeros((M, 8, 128), f32))

    def fix(h):
        backward(h)

    for h in range(H):
        fix(h)
    scatter(S2, R2, k1, 2)

    def store(slot, b, h, value):
        nat[slot, pl.ds(pl.multiple_of(b * 16, 16), 16), pl.ds(h * 1024, 1024)] = value.reshape(
            B, 1024
        ).astype(bf16)

    for h in range(H):

        def early(b, acc):
            at = pl.ds(b * B, B)
            gain = gainv[pl.ds(h * 8, 8), :][None]
            si = RS[at, h] * INVT[at]
            store(0, b, h, si * gain)
            gs = GS[at, h]
            store(4, b, h, gs)
            GF0[at, h] = gs * Y[at, h]
            return acc + jnp.sum(CT[at, h] * si, axis=0)

        T1[50 + h] = lax.fori_loop(0, nb, early, jnp.zeros((8, 128), f32))
    out_copies = [
        pltpu.make_async_copy(nat.at[slot], dst, outsem.at[i])
        for i, (slot, dst) in enumerate(
            ((0, normed_o), (4, gres_o), (1, gq_o), (2, gk_o), (3, gv_o))
        )
    ]
    out_copies[0].start()
    out_copies[1].start()

    def grad_halo(i, ref):
        return pltpu.make_async_remote_copy(
            src_ref=ref.at[pl.ds(0, HALO)], dst_ref=ref.at[pl.ds(rows, HALO)],
            send_sem=hssem.at[3 + i], recv_sem=hrsem.at[3 + i],
            device_id=peer(lax.rem(me + n - 1, n)), device_id_type=MESH,
        )

    grad_copies = [grad_halo(i, ref) for i, ref in enumerate((GF0, GF1, GF2))]

    @pl.when(me > 0)
    def _():
        grad_copies[0].start()

    def correlate(h):
        def step(b, acc):
            u = [U[b * B + t, h] for t in range(B)]
            dz = [DZ[b * B + t, h] for t in range(B)]
            return tuple(
                acc[k] + total(dz[t] * u[t - k] for t in range(k, B)) for k in range(B)
            )

        zero = jnp.zeros((8, 128), f32)
        out = lax.fori_loop(0, nb, step, (zero,) * B)
        for k in range(B):
            CK[h, k] = out[k]

    loop(H, correlate)
    arrived(R2, 2)
    scan(R2, E2, True)
    scatter(E2, A0, k1, 3)

    def inside_back(h):
        def step(b):
            dz = [DZ[b * B + t, h] for t in range(B)]
            kt = [KT[h, k] for k in range(B)]
            for s in range(B):
                G[b * B + s, h] = total(kt[k] * dz[s + k] for k in range(B - s))

        loop(nb, step)

    loop(H, inside_back)

    def mode_sums(h):
        def step(b):
            dz = DZ[pl.ds(b * B, B), h]
            x = XB[h, b]
            RA[h] = RA[h] + x * AB[h, b]
            q = total_in_order([WP[h, s] * dz[s][None] for s in range(1, B)])
            SA[h] = SA[h] + x * q

        RA[h] = jnp.zeros((M, 8, 128), f32)
        SA[h] = jnp.zeros((M, 8, 128), f32)
        loop(nb, step)
        a = AP[h, 1]
        gr = a * RA[h]
        gl = a * SA[h]
        for k in range(B):
            c = CK[h, k][None]
            gr = gr + AP[h, k] * c
            gl = gl + WP[h, k] * c
        T1[pl.ds(h * M, M)] = gr
        SA[h] = gl
        T1[48 + h] = CK[h, 0]

    loop(H, mode_sums)

    def filter_sums(src, gf, dst, base):
        def half(h):
            def step(b, acc):
                win = window(src, b, h)
                g = gf[pl.ds(b * 8, 8), h]
                return tuple(
                    acc[j] + jnp.sum(g * win[HALO - j : HALO - j + 8], axis=0) for j in range(KS)
                )

            zero = jnp.zeros((8, 128), f32)
            out = lax.fori_loop(0, rows // 8, step, (zero,) * KS)
            for j in range(KS):
                dst[base + h * 8 + j] = out[j]
            dst[base + h * 8 + KS] = zero

        loop(H, half)

    filter_sums(QX, GF0, T1, 32)
    T1[pl.ds(48 + 2 + H, 16 - 2 - H)] = jnp.zeros((16 - 2 - H, 8, 128), f32)
    scatter(T1, RR1, k2, 4)

    @pl.when(me == n - 1)
    def _():
        for ref in (GF0, GF1, GF2):
            ref[pl.ds(rows, 8)] = jnp.zeros((8, H, 8, 128), f32)

    @pl.when(me < n - 1)
    def _():
        grad_copies[0].wait_recv()

    def back_filter(gf, i, slot):
        for h in range(H):

            def step(b):
                win = gf[pl.ds(b * B, B + HALO), h]
                store(slot, b, h, total(SW[i, h, j][None] * win[j : j + B] for j in range(KS)))

            loop(nb, step)

    back_filter(GF0, 0, 1)
    out_copies[2].start()
    arrived(A0, 3)

    def exits(h):
        def step(i, x):
            b = nb - 1 - i
            earlier = AP[h, B] * x + AB[h, b]
            AB[h, b] = x
            return earlier

        lax.fori_loop(0, nb, step, A0[pl.ds(h * M, M)])

    loop(H, exits)

    def mixed(b):
        for h in range(H):
            a = AP[h, 1]
            out = AB[h, b]
            SA[h] = SA[h] + out * (PB[h, b] + (float(B) * a) * AP[h, B] * XB[h, b])
            z = RT[h] * a * out
            for i in range(B):
                t = b * B + (B - 1 - i)
                g = G[t, h] + jnp.sum(z, axis=0)
                if i + 1 < B:
                    z = a * z
                GF1[t, h] = g * F2[t, h]
                GF2[t, h] = g * F1[t, h]

    mixed(0)

    @pl.when(me > 0)
    def _():
        grad_copies[1].start()
        grad_copies[2].start()

    loop(nb, mixed, 1)
    arrived(RR1, 4)

    def reduce(src, dst):
        dst[...] = total(src[pl.ds(i * k2, k2)] for i in range(n))

    reduce(RR1, SUM1)
    spread(SUM1, AG1, k2, 5)
    for h in range(H):
        T2[pl.ds(h * M, M)] = -RT[h] * SA[h]
    filter_sums(KX, GF1, T2, 32)
    filter_sums(VX, GF2, T2, 48)
    scatter(T2, RR2, k2, 6)

    @pl.when(me < n - 1)
    def _():
        grad_copies[1].wait_recv()
        grad_copies[2].wait_recv()

    back_filter(GF1, 1, 2)
    out_copies[3].start()
    arrived(RR2, 6)
    reduce(RR2, SUM2)
    spread(SUM2, AG2, k2, 7)
    back_filter(GF2, 2, 3)
    out_copies[4].start()

    def natural(src, at, count):
        return src[pl.ds(at, count)].reshape(count, 1024)

    arrived(AG1, 5)
    for h in range(H):
        cols = pl.ds(h * 1024, 1024)
        grv[:, cols] = natural(AG1, h * M, M)
        shv[0, :, cols] = natural(AG1, 32 + h * 8, 8)[0:KS]
        skipv[pl.ds(h * 8, 8), :] = AG1[48 + h]
        gainv[pl.ds(h * 8, 8), :] = AG1[50 + h]
    arrived(AG2, 7)
    for h in range(H):
        cols = pl.ds(h * 1024, 1024)
        glv[:, cols] = natural(AG2, h * M, M)
        shv[1, :, cols] = natural(AG2, 32 + h * 8, 8)[0:KS]
        shv[2, :, cols] = natural(AG2, 48 + h * 8, 8)[0:KS]
    small = [
        pltpu.make_async_copy(s, d, outsem.at[5 + i])
        for i, (s, d) in enumerate(
            ((shv, short_o), (grv, gr_o), (glv, gl_o), (skipv, gskip_o), (gainv, ggain_o))
        )
    ]
    for copy in small:
        copy.start()

    for at, dst, size in (
        (0, R1, k1), (1, X0, k1), (2, R2, k1), (3, A0, k1),
        (4, RR1, k2), (5, AG1, k2), (6, RR2, k2), (7, AG2, k2),
    ):
        sent(dst, size, at)
    part = tpr.at[pl.ds(0, ntp - 1)]
    pltpu.make_async_copy(part, part, ssem.at[8]).wait()

    @pl.when(me < n - 1)
    def _():
        for copy in halo_copies:
            copy.wait_send()

    @pl.when(me > 0)
    def _():
        for copy in grad_copies:
            copy.wait_send()

    for copy in out_copies + small:
        copy.wait()


def shards(
    n, ntp, residual, query_in, key_in, value_in, short_filter, residues, decay_rate, skip_gain,
    norm_gain, cotangent,
):
    rows, width = residual.shape
    H = width // 1024
    nb = rows // B
    tiles = H * M

    def V(*shape, dtype=f32):
        return pltpu.VMEM(shape, dtype)

    def tm(extra=0):
        return V(rows + extra, H, 8, 128)

    def tile(count):
        return V(count, 8, 128)

    k1, k2 = tiles // n, 64 // n
    scratch = (
        [V(5, rows, width, dtype=bf16), V(3, 16, width, dtype=bf16)]
        + [V(3, KS, width), V(M, width), V(M, width), V(H * 8, 128), V(H * 8, 128)]
        + [tm(8)] * 3 + [tm()] * 10 + [tm(8)] * 3
        + [V(H, B + 1, M, 8, 128)] * 2
        + [V(H, B + 1, 8, 128), V(H, M, 8, 128), V(3, H, 8, 8, 128), tile(tiles)]
        + [V(H, nb, M, 8, 128)] * 3
        + [tile(tiles)] * 8
        + [V(B, 128), V(ntp, B, 128), tile(rows), tile(rows)]
        + [V(H, M, 8, 128), V(H, M, 8, 128), V(H, B, 8, 128), V(8, 1024)]
        + [tile(64), tile(64), tile(k2), tile(64)] * 2
        + [V(3, KS, width), V(M, width), V(M, width)]
        + [pltpu.SemaphoreType.DMA((c,)) for c in (10, 10, 9, 9, 6, 6)]
    )
    big = jax.ShapeDtypeStruct((rows, width), bf16)
    vec = jax.ShapeDtypeStruct((H * 8, 128), f32)
    out_shape = (
        [big] * 5
        + [jax.ShapeDtypeStruct((3, KS, width), f32)]
        + [jax.ShapeDtypeStruct((M, width), f32)] * 2
        + [vec, vec]
    )
    anywhere = pl.BlockSpec(memory_space=pl.ANY)
    outs = pl.pallas_call(
        functools.partial(kernel, n, ntp, rows, width),
        out_shape=out_shape,
        in_specs=[anywhere] * 10,
        out_specs=[anywhere] * 10,
        scratch_shapes=scratch,
        compiler_params=pltpu.CompilerParams(
            collective_id=0, has_side_effects=True, vmem_limit_bytes=60 << 20
        ),
    )(
        residual, query_in, key_in, value_in, short_filter, residues, decay_rate,
        skip_gain.reshape(H * 8, 128), norm_gain.reshape(H * 8, 128), cotangent,
    )
    return (*outs[:8], outs[8].reshape(width), outs[9].reshape(width))


def solution(mesh):
    act, par, vec = P("ctx", "tp"), P(None, "tp"), P("tp")
    short = P(None, None, "tp")
    return jax.shard_map(
        functools.partial(shards, mesh.shape["ctx"], mesh.shape["tp"]),
        mesh=mesh,
        in_specs=(act, act, act, act, short, par, par, vec, vec, act),
        out_specs=(act, act, act, act, act, short, par, par, vec, vec),
        check_vma=False,
    )
```

```python
import functools

import jax
import jax.numpy as jnp
from jax import lax
from jax.experimental import pallas as pl
from jax.experimental.pallas import tpu as pltpu
from jax.sharding import PartitionSpec as P

f32 = jnp.float32
bf16 = jnp.bfloat16
MESH = pl.DeviceIdType.MESH
B = 16
M = 16
KS = 7
HALO = KS - 1


def loop(count, step, start=0):
    def lap(i, carry):
        step(i)
        return carry

    lax.fori_loop(start, count, lap, 0)


def total(terms):
    terms = list(terms)
    while len(terms) > 1:
        terms = [
            terms[i] + terms[i + 1] if i + 1 < len(terms) else terms[i]
            for i in range(0, len(terms), 2)
        ]
    return terms[0]


def kernel(
    n, ntp, rows, width,
    res_h, q_h, k_h, v_h, sf_h, r_h, lam_h, skip_h, gain_h, cot_h,
    normed_o, gres_o, gq_o, gk_o, gv_o, short_o, gr_o, gl_o, gskip_o, ggain_o,
    halo, sfv, rv, lv, skipv, gainv,
    QX, KX, VX, RS, CT, F0, F1, F2, U, Y, DZ, GS, G, GF0, GF1, GF2,
    AP, WP, KT, RT, SW, AT, XB, PB, AB,
    S1, R1, E1, X0, S2, R2, E2, A0,
    sums, tpr, INVT, CFT, RA, SA, CK, SG,
    T1, RR1, SUM1, AG1, T2, RR2, SUM2, AG2,
    insem, ssem, rsem, hssem, hrsem,
):
    H = width // 1024
    nb = rows // B
    D = width * ntp
    me = lax.axis_index("ctx")
    mt = lax.axis_index("tp")
    tiles = H * M
    k1 = tiles // n
    k2 = 64 // n

    def peer(p):
        return (p, mt)

    nat = (normed_o, gq_o, gk_o, gv_o, gres_o)

    ins = [
        (k_h, nat[2]), (v_h, nat[3]), (q_h, nat[1]), (res_h, nat[0]), (cot_h, nat[4]),
        (sf_h, sfv), (r_h, rv), (lam_h, lv), (skip_h, skipv), (gain_h, gainv),
    ]
    in_copies = [pltpu.make_async_copy(s, d, insem.at[i]) for i, (s, d) in enumerate(ins)]
    for copy in in_copies:
        copy.start()

    barrier = pltpu.get_barrier_semaphore()

    def greet(i):
        pl.semaphore_signal(
            barrier, inc=1, device_id=peer(lax.rem(me + i, n)), device_id_type=MESH
        )

    loop(n, greet, 1)
    for i in range(1, ntp):
        pl.semaphore_signal(
            barrier, inc=1, device_id=(me, lax.rem(mt + i, ntp)), device_id_type=MESH
        )
    pl.semaphore_wait(barrier, n - 1 + ntp - 1)

    def in_halo(i, src):
        return pltpu.make_async_remote_copy(
            src_ref=src.at[pl.ds(rows - 16, 16)], dst_ref=halo.at[i],
            send_sem=hssem.at[i], recv_sem=hrsem.at[i],
            device_id=peer(lax.rem(me + 1, n)), device_id_type=MESH,
        )

    halo_copies = [in_halo(0, q_h), in_halo(1, k_h), in_halo(2, v_h)]

    @pl.when(me < n - 1)
    def _():
        for copy in halo_copies:
            copy.start()

    for i in range(5, 10):
        in_copies[i].wait()
    for h in range(H):
        cols = pl.ds(h * 1024, 1024)
        lam = lv[:, cols].reshape(M, 8, 128)
        r = rv[:, cols].reshape(M, 8, 128)
        RT[h] = r
        AT[pl.ds(h * M, M)] = jnp.exp(lam * (-float(rows)))
        for i in range(3):
            SG[0:8, :] = jnp.zeros((8, 1024), f32)
            SG[0:KS, :] = sfv[i, :, cols]
            SW[i, h] = SG[0:8, :].reshape(8, 8, 128)

        def powers(k):
            p = jnp.exp(lam * (-k.astype(f32)))
            AP[h, k] = p
            WP[h, k] = p * k.astype(f32)
            KT[h, k] = jnp.sum(r * p, axis=0)

        loop(B + 1, powers)
        KT[h, 0] = KT[h, 0] + skipv[pl.ds(h * 8, 8), :]

    def to_tm(slot, dst, off):
        def step(i):
            v = nat[slot][pl.ds(pl.multiple_of(i * 16, 16), 16), :].astype(f32)
            dst[pl.ds(off + i * 16, 16)] = v.reshape(16, H, 8, 128)

        loop(rows // 16, step)

    in_copies[0].wait()
    to_tm(2, KX, 8)
    in_copies[1].wait()
    to_tm(3, VX, 8)
    in_copies[2].wait()
    to_tm(1, QX, 8)

    @pl.when(me > 0)
    def _():
        for copy in halo_copies:
            copy.wait_recv()

    @pl.when(me == 0)
    def _():
        halo[...] = jnp.zeros(halo.shape, bf16)

    for i, dst in enumerate((QX, KX, VX)):
        dst[pl.ds(0, 8)] = halo[i].astype(f32)[8:16].reshape(8, H, 8, 128)

    def window(src, b, h):
        return src[pl.ds(b * 8 + 2, 14), h]

    def fir(win, i, h):
        return total(SW[i, h, j][None] * win[HALO - j : HALO - j + 8] for j in range(KS))

    def feature(h):
        def step(b):
            at = pl.ds(b * 8, 8)
            f1 = fir(window(KX, b, h), 1, h)
            F1[at, h] = f1
            f2 = fir(window(VX, b, h), 2, h)
            F2[at, h] = f2
            U[at, h] = f1 * f2

        loop(rows // 8, step)

    loop(H, feature)

    def summary(h):
        a = AP[h, 1]

        def step(b, run):
            u = U[pl.ds(b * B, B), h]
            x = a * u[0][None] + u[1][None]
            for s in range(2, B):
                x = a * x + u[s][None]
            XB[h, b] = x
            return AP[h, B] * run + x

        S1[pl.ds(h * M, M)] = lax.fori_loop(0, nb, step, jnp.zeros((M, 8, 128), f32))

    loop(H, summary)

    def scatter(src, dst, size, at):
        def step(i):
            p = lax.rem(me + i, n)
            pltpu.make_async_remote_copy(
                src_ref=src.at[pl.ds(p * size, size)], dst_ref=dst.at[pl.ds(me * size, size)],
                send_sem=ssem.at[at], recv_sem=rsem.at[at],
                device_id=peer(p), device_id_type=MESH,
            ).start()

        loop(n, step, 1)
        mine = pl.ds(me * size, size)
        pltpu.make_async_copy(src.at[mine], dst.at[mine], rsem.at[at]).start()

    def spread(src, dst, size, at):
        mine = pl.ds(me * size, size)

        def step(i):
            p = lax.rem(me + i, n)
            pltpu.make_async_remote_copy(
                src_ref=src, dst_ref=dst.at[mine],
                send_sem=ssem.at[at], recv_sem=rsem.at[at],
                device_id=peer(p), device_id_type=MESH,
            ).start()

        loop(n, step, 1)
        pltpu.make_async_copy(src, dst.at[mine], rsem.at[at]).start()

    def arrived(dst, at):
        pltpu.make_async_copy(dst, dst, rsem.at[at]).wait()

    def sent(dst, size, at):
        part = dst.at[pl.ds(0, (n - 1) * size)]
        pltpu.make_async_copy(part, part, ssem.at[at]).wait()

    def scan(src, dst, backward):
        a = AT[pl.ds(me * k1, k1)]
        run = jnp.zeros((k1, 8, 128), f32)
        for i in range(n):
            d = n - 1 - i if backward else i
            at = pl.ds(d * k1, k1)
            dst[at] = run
            run = a * run + src[at]

    scatter(S1, R1, k1, 0)

    def feature_q(h):
        def step(b):
            F0[pl.ds(b * 8, 8), h] = fir(window(QX, b, h), 0, h)

        loop(rows // 8, step)

    loop(H, feature_q)

    def inside(h):
        def step(b):
            u = [U[b * B + t, h] for t in range(B)]
            kt = [KT[h, k] for k in range(B)]
            for t in range(B):
                Y[b * B + t, h] = total(kt[k] * u[t - k] for k in range(t + 1))

        loop(nb, step)

    loop(H, inside)
    arrived(R1, 0)
    scan(R1, E1, False)
    scatter(E1, X0, k1, 1)

    def weighted(h):
        def step(b):
            u = U[pl.ds(b * B, B), h]
            PB[h, b] = total_in_order([WP[h, B - s] * u[s][None] for s in range(B)])

        loop(nb, step)

    def total_in_order(terms):
        out = terms[0]
        for term in terms[1:]:
            out = out + term
        return out

    loop(H, weighted)
    in_copies[3].wait()
    to_tm(0, RS, 0)
    in_copies[4].wait()
    to_tm(4, CT, 0)
    arrived(X0, 1)

    def entry(h):
        def step(b, x):
            later = AP[h, B] * x + XB[h, b]
            XB[h, b] = x
            return later

        lax.fori_loop(0, nb, step, X0[pl.ds(h * M, M)])

    loop(H, entry)

    lane = lax.broadcasted_iota(jnp.int32, (B, 128), 1)
    sums[...] = jnp.zeros((B, 128), f32)

    def forward(b):
        squares = [None] * B
        inner = [None] * B
        for h in range(H):
            a = AP[h, 1]
            z = RT[h] * a * XB[h, b]
            gain = gainv[pl.ds(h * 8, 8), :]
            for i in range(B):
                t = b * B + i
                y = Y[t, h] + jnp.sum(z, axis=0)
                if i + 1 < B:
                    z = a * z
                Y[t, h] = y
                s = RS[t, h] + F0[t, h] * y
                RS[t, h] = s
                sq = s * s
                ip = CT[t, h] * gain * s
                squares[i] = sq if h == 0 else squares[i] + sq
                inner[i] = ip if h == 0 else inner[i] + ip

        def column(parts):
            return jnp.sum(jnp.stack(parts).reshape(B, 1024), axis=1, keepdims=True)

        now = jnp.where(lane == b, column(squares), sums[...])
        sums[...] = jnp.where(lane == nb + b, column(inner), now)

    loop(nb, forward)
    for i in range(1, ntp):
        p = lax.rem(mt + i, ntp)
        pltpu.make_async_remote_copy(
            src_ref=sums, dst_ref=tpr.at[mt], send_sem=ssem.at[8], recv_sem=rsem.at[8],
            device_id=(me, p), device_id_type=MESH,
        ).start()
    pltpu.make_async_copy(sums, tpr.at[mt], rsem.at[8]).start()
    pltpu.make_async_copy(tpr, tpr, rsem.at[8]).wait()
    tot = total(tpr[i] for i in range(ntp))
    inner_sum = pltpu.roll(tot, 128 - nb, 1)
    valid = lane < nb
    inv_all = lax.rsqrt(jnp.where(valid, tot, 1.0) / D + 1e-5)
    coef_all = inv_all * inv_all * inv_all * jnp.where(valid, inner_sum, 0.0) / D

    def spread_rows(b):
        at = pl.ds(b * B, B)
        for src, dst in ((inv_all, INVT), (coef_all, CFT)):
            col = jnp.sum(jnp.where(lane == b, src, 0.0), axis=1, keepdims=True)
            full = jnp.broadcast_to(col, (B, 128))
            dst[at] = jnp.broadcast_to(full[:, None, :], (B, 8, 128))

    loop(nb, spread_rows)

    def backward(h):
        a = AP[h, 1]

        def step(i, run):
            b = nb - 1 - i
            at = pl.ds(b * B, B)
            gain = gainv[pl.ds(h * 8, 8), :][None]
            gs = INVT[at] * (CT[at, h] * gain) - RS[at, h] * CFT[at]
            GS[at, h] = gs
            dz = gs * F0[at, h]
            DZ[at, h] = dz
            v = a * dz[B - 1][None] + dz[B - 2][None]
            for s in range(B - 3, -1, -1):
                v = a * v + dz[s][None]
            AB[h, b] = v
            return AP[h, B] * run + v

        S2[pl.ds(h * M, M)] = lax.fori_loop(0, nb, step, jnp.zeros((M, 8, 128), f32))

    def fix(h):
        backward(h)

    for h in range(H):
        fix(h)
    scatter(S2, R2, k1, 2)

    def store(slot, b, h, value):
        nat[slot][pl.ds(pl.multiple_of(b * 16, 16), 16), pl.ds(h * 1024, 1024)] = value.reshape(
            B, 1024
        ).astype(bf16)

    for h in range(H):

        def early(b, acc):
            at = pl.ds(b * B, B)
            gain = gainv[pl.ds(h * 8, 8), :][None]
            si = RS[at, h] * INVT[at]
            store(0, b, h, si * gain)
            gs = GS[at, h]
            store(4, b, h, gs)
            GF0[at, h] = gs * Y[at, h]
            return acc + jnp.sum(CT[at, h] * si, axis=0)

        T1[50 + h] = lax.fori_loop(0, nb, early, jnp.zeros((8, 128), f32))
    def grad_halo(i, ref):
        return pltpu.make_async_remote_copy(
            src_ref=ref.at[pl.ds(0, HALO)], dst_ref=ref.at[pl.ds(rows, HALO)],
            send_sem=hssem.at[3 + i], recv_sem=hrsem.at[3 + i],
            device_id=peer(lax.rem(me + n - 1, n)), device_id_type=MESH,
        )

    grad_copies = [grad_halo(i, ref) for i, ref in enumerate((GF0, GF1, GF2))]

    @pl.when(me > 0)
    def _():
        grad_copies[0].start()

    def correlate(h):
        def step(b, acc):
            u = [U[b * B + t, h] for t in range(B)]
            dz = [DZ[b * B + t, h] for t in range(B)]
            return tuple(
                acc[k] + total(dz[t] * u[t - k] for t in range(k, B)) for k in range(B)
            )

        zero = jnp.zeros((8, 128), f32)
        out = lax.fori_loop(0, nb, step, (zero,) * B)
        for k in range(B):
            CK[h, k] = out[k]

    loop(H, correlate)
    arrived(R2, 2)
    scan(R2, E2, True)
    scatter(E2, A0, k1, 3)

    def inside_back(h):
        def step(b):
            dz = [DZ[b * B + t, h] for t in range(B)]
            kt = [KT[h, k] for k in range(B)]
            for s in range(B):
                G[b * B + s, h] = total(kt[k] * dz[s + k] for k in range(B - s))

        loop(nb, step)

    loop(H, inside_back)

    def mode_sums(h):
        def step(b):
            dz = DZ[pl.ds(b * B, B), h]
            x = XB[h, b]
            RA[h] = RA[h] + x * AB[h, b]
            q = total_in_order([WP[h, s] * dz[s][None] for s in range(1, B)])
            SA[h] = SA[h] + x * q

        RA[h] = jnp.zeros((M, 8, 128), f32)
        SA[h] = jnp.zeros((M, 8, 128), f32)
        loop(nb, step)
        a = AP[h, 1]
        gr = a * RA[h]
        gl = a * SA[h]
        for k in range(B):
            c = CK[h, k][None]
            gr = gr + AP[h, k] * c
            gl = gl + WP[h, k] * c
        T1[pl.ds(h * M, M)] = gr
        SA[h] = gl
        T1[48 + h] = CK[h, 0]

    loop(H, mode_sums)

    def filter_sums(src, gf, dst, base):
        def half(h):
            def step(b, acc):
                win = window(src, b, h)
                g = gf[pl.ds(b * 8, 8), h]
                return tuple(
                    acc[j] + jnp.sum(g * win[HALO - j : HALO - j + 8], axis=0) for j in range(KS)
                )

            zero = jnp.zeros((8, 128), f32)
            out = lax.fori_loop(0, rows // 8, step, (zero,) * KS)
            for j in range(KS):
                dst[base + h * 8 + j] = out[j]
            dst[base + h * 8 + KS] = zero

        loop(H, half)

    filter_sums(QX, GF0, T1, 32)
    T1[pl.ds(48 + 2 + H, 16 - 2 - H)] = jnp.zeros((16 - 2 - H, 8, 128), f32)
    scatter(T1, RR1, k2, 4)

    @pl.when(me == n - 1)
    def _():
        for ref in (GF0, GF1, GF2):
            ref[pl.ds(rows, 8)] = jnp.zeros((8, H, 8, 128), f32)

    @pl.when(me < n - 1)
    def _():
        grad_copies[0].wait_recv()

    def back_filter(gf, i, slot):
        for h in range(H):

            def step(b):
                win = gf[pl.ds(b * B, B + HALO), h]
                store(slot, b, h, total(SW[i, h, j][None] * win[j : j + B] for j in range(KS)))

            loop(nb, step)

    back_filter(GF0, 0, 1)
    arrived(A0, 3)

    def exits(h):
        def step(i, x):
            b = nb - 1 - i
            earlier = AP[h, B] * x + AB[h, b]
            AB[h, b] = x
            return earlier

        lax.fori_loop(0, nb, step, A0[pl.ds(h * M, M)])

    loop(H, exits)

    def mixed(b):
        for h in range(H):
            a = AP[h, 1]
            out = AB[h, b]
            SA[h] = SA[h] + out * (PB[h, b] + (float(B) * a) * AP[h, B] * XB[h, b])
            z = RT[h] * a * out
            for i in range(B):
                t = b * B + (B - 1 - i)
                g = G[t, h] + jnp.sum(z, axis=0)
                if i + 1 < B:
                    z = a * z
                GF1[t, h] = g * F2[t, h]
                GF2[t, h] = g * F1[t, h]

    mixed(0)

    @pl.when(me > 0)
    def _():
        grad_copies[1].start()
        grad_copies[2].start()

    loop(nb, mixed, 1)
    arrived(RR1, 4)

    def reduce(src, dst):
        dst[...] = total(src[pl.ds(i * k2, k2)] for i in range(n))

    reduce(RR1, SUM1)
    spread(SUM1, AG1, k2, 5)
    for h in range(H):
        T2[pl.ds(h * M, M)] = -RT[h] * SA[h]
    filter_sums(KX, GF1, T2, 32)
    filter_sums(VX, GF2, T2, 48)
    scatter(T2, RR2, k2, 6)

    @pl.when(me < n - 1)
    def _():
        grad_copies[1].wait_recv()
        grad_copies[2].wait_recv()

    back_filter(GF1, 1, 2)
    arrived(RR2, 6)
    reduce(RR2, SUM2)
    spread(SUM2, AG2, k2, 7)
    back_filter(GF2, 2, 3)

    def natural(src, at, count):
        return src[pl.ds(at, count)].reshape(count, 1024)

    arrived(AG1, 5)
    for h in range(H):
        cols = pl.ds(h * 1024, 1024)
        gr_o[:, cols] = natural(AG1, h * M, M)
        short_o[0, :, cols] = natural(AG1, 32 + h * 8, 8)[0:KS]
        gskip_o[pl.ds(h * 8, 8), :] = AG1[48 + h]
        ggain_o[pl.ds(h * 8, 8), :] = AG1[50 + h]
    arrived(AG2, 7)
    for h in range(H):
        cols = pl.ds(h * 1024, 1024)
        gl_o[:, cols] = natural(AG2, h * M, M)
        short_o[1, :, cols] = natural(AG2, 32 + h * 8, 8)[0:KS]
        short_o[2, :, cols] = natural(AG2, 48 + h * 8, 8)[0:KS]

    for at, dst, size in (
        (0, R1, k1), (1, X0, k1), (2, R2, k1), (3, A0, k1),
        (4, RR1, k2), (5, AG1, k2), (6, RR2, k2), (7, AG2, k2),
    ):
        sent(dst, size, at)
    part = tpr.at[pl.ds(0, ntp - 1)]
    pltpu.make_async_copy(part, part, ssem.at[8]).wait()

    @pl.when(me < n - 1)
    def _():
        for copy in halo_copies:
            copy.wait_send()

    @pl.when(me > 0)
    def _():
        for copy in grad_copies:
            copy.wait_send()


def deliver(*refs):
    ins, outs, sem = refs[:10], refs[10:20], refs[20]
    copies = [pltpu.make_async_copy(s, d, sem.at[i]) for i, (s, d) in enumerate(zip(ins, outs))]
    for copy in copies:
        copy.start()
    for copy in copies:
        copy.wait()


def shards(
    n, ntp, residual, query_in, key_in, value_in, short_filter, residues, decay_rate, skip_gain,
    norm_gain, cotangent,
):
    rows, width = residual.shape
    H = width // 1024
    nb = rows // B
    tiles = H * M

    def V(*shape, dtype=f32):
        return pltpu.VMEM(shape, dtype)

    def tm(extra=0):
        return V(rows + extra, H, 8, 128)

    def tile(count):
        return V(count, 8, 128)

    k1, k2 = tiles // n, 64 // n
    scratch = (
        [V(3, 16, width, dtype=bf16)]
        + [V(3, KS, width), V(M, width), V(M, width), V(H * 8, 128), V(H * 8, 128)]
        + [tm(8)] * 3 + [tm()] * 10 + [tm(8)] * 3
        + [V(H, B + 1, M, 8, 128)] * 2
        + [V(H, B + 1, 8, 128), V(H, M, 8, 128), V(3, H, 8, 8, 128), tile(tiles)]
        + [V(H, nb, M, 8, 128)] * 3
        + [tile(tiles)] * 8
        + [V(B, 128), V(ntp, B, 128), tile(rows), tile(rows)]
        + [V(H, M, 8, 128), V(H, M, 8, 128), V(H, B, 8, 128), V(8, 1024)]
        + [tile(64), tile(64), tile(k2), tile(64)] * 2
        + [pltpu.SemaphoreType.DMA((c,)) for c in (10, 9, 9, 6, 6)]
    )
    big = jax.ShapeDtypeStruct((rows, width), bf16)
    vec = jax.ShapeDtypeStruct((H * 8, 128), f32)
    out_shape = (
        [big] * 5
        + [jax.ShapeDtypeStruct((3, KS, width), f32)]
        + [jax.ShapeDtypeStruct((M, width), f32)] * 2
        + [vec, vec]
    )
    anywhere = pl.BlockSpec(memory_space=pl.ANY)
    outs = pl.pallas_call(
        functools.partial(kernel, n, ntp, rows, width),
        out_shape=[V(*o.shape, dtype=o.dtype) for o in out_shape],
        in_specs=[anywhere] * 10,
        out_specs=[pl.BlockSpec(memory_space=pltpu.VMEM)] * 10,
        scratch_shapes=scratch,
        compiler_params=pltpu.CompilerParams(
            collective_id=0, has_side_effects=True, vmem_limit_bytes=52 << 20
        ),
    )(
        residual, query_in, key_in, value_in, short_filter, residues, decay_rate,
        skip_gain.reshape(H * 8, 128), norm_gain.reshape(H * 8, 128), cotangent,
    )
    outs = pl.pallas_call(
        deliver,
        out_shape=out_shape,
        in_specs=[anywhere] * 10,
        out_specs=[anywhere] * 10,
        scratch_shapes=[pltpu.SemaphoreType.DMA((10,))],
        compiler_params=pltpu.CompilerParams(vmem_limit_bytes=1 << 20),
    )(*outs)
    return (*outs[:8], outs[8].reshape(width), outs[9].reshape(width))


def solution(mesh):
    act, par, vec = P("ctx", "tp"), P(None, "tp"), P("tp")
    short = P(None, None, "tp")
    return jax.shard_map(
        functools.partial(shards, mesh.shape["ctx"], mesh.shape["tp"]),
        mesh=mesh,
        in_specs=(act, act, act, act, short, par, par, vec, vec, act),
        out_specs=(act, act, act, act, act, short, par, par, vec, vec),
        check_vma=False,
    )
```

```python
import functools

import jax
import jax.numpy as jnp
from jax import lax
from jax.experimental import pallas as pl
from jax.experimental.pallas import tpu as pltpu
from jax.sharding import PartitionSpec as P

f32 = jnp.float32
bf16 = jnp.bfloat16
MESH = pl.DeviceIdType.MESH
B = 16
M = 16
KS = 7
HALO = KS - 1


def loop(count, step, start=0):
    def lap(i, carry):
        step(i)
        return carry

    lax.fori_loop(start, count, lap, 0)


def total(terms):
    terms = list(terms)
    while len(terms) > 1:
        terms = [
            terms[i] + terms[i + 1] if i + 1 < len(terms) else terms[i]
            for i in range(0, len(terms), 2)
        ]
    return terms[0]


def kernel(
    n, ntp, rows, width,
    res_h, q_h, k_h, v_h, sf_h, r_h, lam_h, skip_h, gain_h, cot_h,
    normed_o, gres_o, gq_o, gk_o, gv_o, short_o, gr_o, gl_o, gskip_o, ggain_o,
    halo, sfv, rv, lv, skipv, gainv,
    QX, KX, VX, RS, CT, F0, F1, F2, U, Y, DZ, GS, G, GF0, GF1, GF2,
    AP, WP, KT, RT, LM, SW, AT, XB, PB, AB,
    S1, R1, E1, X0, S2, R2, E2, A0,
    sums, tpr, INVT, CFT, RA, SA, QA, CK, SG,
    T1, RR1, SUM1, AG1, T2, RR2, SUM2, AG2,
    insem, ssem, rsem, hssem, hrsem,
):
    H = width // 1024
    nb = rows // B
    D = width * ntp
    me = lax.axis_index("ctx")
    mt = lax.axis_index("tp")
    tiles = H * M
    k1 = tiles // n
    k2 = 64 // n
    k3 = 32 // n

    def peer(p):
        return (p, mt)

    nat = (normed_o, gq_o, gk_o, gv_o, gres_o)

    ins = [
        (lam_h, lv), (sf_h, sfv), (k_h, nat[2]), (v_h, nat[3]), (r_h, rv), (skip_h, skipv),
        (gain_h, gainv), (q_h, nat[1]), (res_h, nat[0]), (cot_h, nat[4]),
    ]
    in_copies = [pltpu.make_async_copy(s, d, insem.at[i]) for i, (s, d) in enumerate(ins)]
    for copy in in_copies:
        copy.start()

    barrier = pltpu.get_barrier_semaphore()

    for i in range(1, n):
        pl.semaphore_signal(
            barrier, inc=1, device_id=peer(lax.rem(me + i, n)), device_id_type=MESH
        )
    for i in range(1, ntp):
        pl.semaphore_signal(
            barrier, inc=1, device_id=(me, lax.rem(mt + i, ntp)), device_id_type=MESH
        )

    in_copies[0].wait()
    in_copies[1].wait()
    for h in range(H):
        cols = pl.ds(h * 1024, 1024)
        lam = lv[:, cols].reshape(M, 8, 128)
        AP[h, 1] = jnp.exp(-lam)
        AP[h, B] = jnp.exp(lam * (-float(B)))
        LM[h] = lam
        AT[pl.ds(h * M, M)] = jnp.exp(lam * (-float(rows)))
        for i in range(3):
            SG[0:8, :] = jnp.zeros((8, 1024), f32)
            SG[0:KS, :] = sfv[i, :, cols]
            SW[i, h] = SG[0:8, :].reshape(8, 8, 128)

    def to_tm(slot, dst, off):
        def step(i):
            v = nat[slot][pl.ds(pl.multiple_of(i * 16, 16), 16), :].astype(f32)
            dst[pl.ds(off + i * 16, 16)] = v.reshape(16, H, 8, 128)

        loop(rows // 16, step)

    in_copies[2].wait()
    to_tm(2, KX, 8)
    in_copies[3].wait()
    to_tm(3, VX, 8)

    pl.semaphore_wait(barrier, n - 1 + ntp - 1)

    def in_halo(i, src):
        return pltpu.make_async_remote_copy(
            src_ref=src.at[pl.ds(rows - 16, 16)], dst_ref=halo.at[i],
            send_sem=hssem.at[i], recv_sem=hrsem.at[i],
            device_id=peer(lax.rem(me + 1, n)), device_id_type=MESH,
        )

    halo_copies = [in_halo(0, q_h), in_halo(1, k_h), in_halo(2, v_h)]

    @pl.when(me < n - 1)
    def _():
        for i in (1, 2, 0):
            halo_copies[i].start()

    def window(src, b, h):
        return src[pl.ds(b * 8 + 2, 14), h]

    def fir(win, i, h):
        return total(SW[i, h, j][None] * win[HALO - j : HALO - j + 8] for j in range(KS))

    def feature(h, b):
        at = pl.ds(b * 8, 8)
        f1 = fir(window(KX, b, h), 1, h)
        F1[at, h] = f1
        f2 = fir(window(VX, b, h), 2, h)
        F2[at, h] = f2
        U[at, h] = f1 * f2

    def gather(h, b):
        a = AP[h, 1]
        u = U[pl.ds(b * B, B), h]
        x = a * u[0][None] + u[1][None]
        for s in range(2, B):
            x = a * x + u[s][None]
        XB[h, b] = x
        return x

    def summary(h):
        def step(b, run):
            return AP[h, B] * run + gather(h, b)

        S1[pl.ds(h * M, M)] = lax.fori_loop(1, nb, step, jnp.zeros((M, 8, 128), f32))

    for h in range(H):
        loop(rows // 8, functools.partial(feature, h), 1)
    loop(H, summary)

    @pl.when(me > 0)
    def _():
        for i in (1, 2, 0):
            halo_copies[i].wait_recv()

    @pl.when(me == 0)
    def _():
        halo[...] = jnp.zeros(halo.shape, bf16)

    for i, dst in enumerate((QX, KX, VX)):
        dst[pl.ds(0, 8)] = halo[i].astype(f32)[8:16].reshape(8, H, 8, 128)

    half = n // H

    def remote(src, dst, p, at):
        pltpu.make_async_remote_copy(
            src_ref=src, dst_ref=dst, send_sem=ssem.at[at[0]], recv_sem=rsem.at[at[1]],
            device_id=peer(p), device_id_type=MESH,
        ).start()

    def part(ref, p, size):
        return ref.at[pl.ds(p * size, size)]

    def scatter(src, dst, size, at):
        mine = part(dst, me, size)
        for i in range(1, n):
            p = lax.rem(me + i, n)
            remote(part(src, p, size), mine, p, at)
        pltpu.make_async_copy(part(src, me, size), mine, rsem.at[at[1]]).start()

    def scatter_half(src, dst, size, at, h):
        mine = part(dst, me, size)
        for i in range(1, half):
            p = h * half + lax.rem(me + i, half)
            remote(part(src, p, size), mine, p, at)
        first = me < half if h == 0 else me >= half
        other = me >= half if h == 0 else me < half

        @pl.when(first)
        def _():
            pltpu.make_async_copy(part(src, me, size), mine, rsem.at[at[1]]).start()

        @pl.when(other)
        def _():
            p = h * half + lax.rem(me, half)
            remote(part(src, p, size), mine, p, at)

    def spread(src, dst, size, at):
        mine = part(dst, me, size)
        for i in range(1, n):
            remote(src, mine, lax.rem(me + i, n), at)
        pltpu.make_async_copy(src, mine, rsem.at[at[1]]).start()

    def arrived(dst, at):
        pltpu.make_async_copy(dst, dst, rsem.at[at]).wait()

    def sent(dst, size, at):
        all_but_one = dst.at[pl.ds(0, (n - 1) * size)]
        pltpu.make_async_copy(all_but_one, all_but_one, ssem.at[at]).wait()

    def scan(src, dst, backward):
        a = AT[pl.ds(me * k1, k1)]
        run = jnp.zeros((k1, 8, 128), f32)
        for i in range(n):
            d = n - 1 - i if backward else i
            at = pl.ds(d * k1, k1)
            dst[at] = run
            run = a * run + src[at]

    def relay(src, mid, dst, at, backward, h):
        @pl.when(me < half if h == 0 else me >= half)
        def _():
            arrived(src, at[1])
            scan(src, mid, backward)
            scatter(mid, dst, k1, (at[0] + 1, at[1] + 1 + h))

    for h in range(H):
        feature(h, 0)
        S1[pl.ds(h * M, M)] = S1[pl.ds(h * M, M)] + gather(h, 0) * jnp.exp(
            LM[h] * (-float(rows - B))
        )
        scatter_half(S1, R1, k1, (0, 0), h)

    for i in (4, 5, 6):
        in_copies[i].wait()
    for h in range(H):
        r = rv[:, pl.ds(h * 1024, 1024)].reshape(M, 8, 128)
        RT[h] = r

        def powers(k):
            p = jnp.exp(LM[h] * (-k.astype(f32)))
            AP[h, k] = p
            WP[h, k] = p * k.astype(f32)
            KT[h, k] = jnp.sum(r * p, axis=0)

        loop(B + 1, powers)
        KT[h, 0] = KT[h, 0] + skipv[pl.ds(h * 8, 8), :]
        RA[h] = r * AP[h, 1]

    def inside(h):
        def step(b):
            u = [U[b * B + t, h] for t in range(B)]
            kt = [KT[h, k] for k in range(B)]
            for t in range(B):
                Y[b * B + t, h] = total(kt[k] * u[t - k] for k in range(t + 1))

        loop(nb, step)

    loop(H, inside)
    in_copies[7].wait()
    to_tm(1, QX, 8)
    relay(R1, E1, X0, (0, 0), False, 0)
    relay(R1, E1, X0, (0, 0), False, 1)

    def feature_q(h):
        def step(b):
            F0[pl.ds(b * 8, 8), h] = fir(window(QX, b, h), 0, h)

        loop(rows // 8, step)

    loop(H, feature_q)
    in_copies[8].wait()
    to_tm(0, RS, 0)
    in_copies[9].wait()
    to_tm(4, CT, 0)

    def total_in_order(terms):
        out = terms[0]
        for term in terms[1:]:
            out = out + term
        return out

    def weighted(h):
        edge = (float(B) * AP[h, 1]) * AP[h, B]

        def step(b):
            u = U[pl.ds(b * B, B), h]
            PB[h, b] = total_in_order(
                [edge * XB[h, b]] + [WP[h, B - s] * u[s][None] for s in range(B)]
            )

        loop(nb, step)

    lane = lax.broadcasted_iota(jnp.int32, (B, 128), 1)
    sums[...] = jnp.zeros((B, 128), f32)

    def column(parts):
        return jnp.sum(jnp.stack(parts).reshape(B, 1024), axis=1, keepdims=True)

    def forward(h, b, x):
        a = AP[h, 1]
        z = RA[h] * x
        later = AP[h, B] * x + XB[h, b]
        XB[h, b] = x
        gain = gainv[pl.ds(h * 8, 8), :]
        squares, inner = [], []
        for i in range(B):
            t = b * B + i
            y = Y[t, h] + jnp.sum(z, axis=0)
            if i + 1 < B:
                z = a * z
            Y[t, h] = y
            s = RS[t, h] + F0[t, h] * y
            RS[t, h] = s
            squares.append(s * s)
            inner.append(CT[t, h] * gain * s)
            if h > 0:
                squares[i] = squares[i] + G[t, 0]
                inner[i] = inner[i] + GS[t, 0]
            if h < H - 1:
                G[t, 0] = squares[i]
                GS[t, 0] = inner[i]
        if h == H - 1:
            now = jnp.where(lane == b, column(squares), sums[...])
            sums[...] = jnp.where(lane == nb + b, column(inner), now)
        return later

    for h in range(H):
        arrived(X0.at[pl.ds(h * M, M)], 1 + h)
        lax.fori_loop(0, nb, functools.partial(forward, h), X0[pl.ds(h * M, M)])
    for i in range(1, ntp):
        p = lax.rem(mt + i, ntp)
        pltpu.make_async_remote_copy(
            src_ref=sums, dst_ref=tpr.at[mt], send_sem=ssem.at[10], recv_sem=rsem.at[12],
            device_id=(me, p), device_id_type=MESH,
        ).start()
    pltpu.make_async_copy(sums, tpr.at[mt], rsem.at[12]).start()
    loop(H, weighted)
    arrived(tpr, 12)
    tot = total(tpr[i] for i in range(ntp))
    inner_sum = pltpu.roll(tot, 128 - nb, 1)
    valid = lane < nb
    inv_all = lax.rsqrt(jnp.where(valid, tot, 1.0) / D + 1e-5)
    coef_all = inv_all * inv_all * inv_all * jnp.where(valid, inner_sum, 0.0) / D

    def spread_rows(b):
        at = pl.ds(b * B, B)
        for src, dst in ((inv_all, INVT), (coef_all, CFT)):
            col = jnp.sum(jnp.where(lane == b, src, 0.0), axis=1, keepdims=True)
            full = jnp.broadcast_to(col, (B, 128))
            dst[at] = jnp.broadcast_to(full[:, None, :], (B, 8, 128))

    loop(nb, spread_rows)

    def backward(h):
        a = AP[h, 1]

        def step(i, run):
            b = nb - 1 - i
            at = pl.ds(b * B, B)
            gain = gainv[pl.ds(h * 8, 8), :][None]
            gs = INVT[at] * (CT[at, h] * gain) - RS[at, h] * CFT[at]
            GS[at, h] = gs
            dz = gs * F0[at, h]
            DZ[at, h] = dz
            v = a * dz[B - 1][None] + dz[B - 2][None]
            for s in range(B - 3, -1, -1):
                v = a * v + dz[s][None]
            AB[h, b] = v
            return AP[h, B] * run + v

        S2[pl.ds(h * M, M)] = lax.fori_loop(0, nb, step, jnp.zeros((M, 8, 128), f32))

    for h in range(H):
        backward(h)
        scatter_half(S2, R2, k1, (2, 3), h)

    def store(slot, b, h, value):
        nat[slot][pl.ds(pl.multiple_of(b * 16, 16), 16), pl.ds(h * 1024, 1024)] = value.reshape(
            B, 1024
        ).astype(bf16)

    for h in range(H):

        def early(b, acc):
            at = pl.ds(b * B, B)
            GF0[at, h] = GS[at, h] * Y[at, h]
            return acc + jnp.sum(CT[at, h] * (RS[at, h] * INVT[at]), axis=0)

        T1[50 + h] = lax.fori_loop(0, nb, early, jnp.zeros((8, 128), f32))

    def grad_halo(i, ref):
        return pltpu.make_async_remote_copy(
            src_ref=ref.at[pl.ds(0, HALO)], dst_ref=ref.at[pl.ds(rows, HALO)],
            send_sem=hssem.at[3 + i], recv_sem=hrsem.at[3 + i],
            device_id=peer(lax.rem(me + n - 1, n)), device_id_type=MESH,
        )

    grad_copies = [grad_halo(i, ref) for i, ref in enumerate((GF0, GF1, GF2))]

    @pl.when(me > 0)
    def _():
        grad_copies[0].start()

    def correlate(h):
        def step(b, acc):
            u = [U[b * B + t, h] for t in range(B)]
            dz = [DZ[b * B + t, h] for t in range(B)]
            return tuple(
                acc[k] + total(dz[t] * u[t - k] for t in range(k, B)) for k in range(B)
            )

        zero = jnp.zeros((8, 128), f32)
        out = lax.fori_loop(0, nb, step, (zero,) * B)
        for k in range(B):
            CK[h, k] = out[k]

    loop(H, correlate)
    def inside_back(h):
        def step(b):
            dz = [DZ[b * B + t, h] for t in range(B)]
            kt = [KT[h, k] for k in range(B)]
            for s in range(B):
                G[b * B + s, h] = total(kt[k] * dz[s + k] for k in range(B - s))

        loop(nb, step)

    loop(H, inside_back)
    relay(R2, E2, A0, (2, 3), True, 0)
    relay(R2, E2, A0, (2, 3), True, 1)

    def mode_sums(h):
        def step(b):
            dz = DZ[pl.ds(b * B, B), h]
            x = XB[h, b]
            QA[h] = QA[h] + x * AB[h, b]
            q = total_in_order([WP[h, s] * dz[s][None] for s in range(1, B)])
            SA[h] = SA[h] + x * q

        QA[h] = jnp.zeros((M, 8, 128), f32)
        SA[h] = jnp.zeros((M, 8, 128), f32)
        loop(nb, step)
        a = AP[h, 1]
        gr = a * QA[h]
        gl = a * SA[h]
        for k in range(B):
            c = CK[h, k][None]
            gr = gr + AP[h, k] * c
            gl = gl + WP[h, k] * c
        T1[pl.ds(h * M, M)] = gr
        SA[h] = gl
        T1[48 + h] = CK[h, 0]

    loop(H, mode_sums)

    def filter_sums(h, src, gf, dst, base):
        def step(b, acc):
            win = window(src, b, h)
            g = gf[pl.ds(b * 8, 8), h]
            return tuple(
                acc[j] + jnp.sum(g * win[HALO - j : HALO - j + 8], axis=0) for j in range(KS)
            )

        zero = jnp.zeros((8, 128), f32)
        out = lax.fori_loop(0, rows // 8, step, (zero,) * KS)
        for j in range(KS):
            dst[base + j] = out[j]
        dst[base + KS] = zero

    for h in range(H):
        filter_sums(h, QX, GF0, T1, 32 + h * 8)
    T1[pl.ds(48 + 2 + H, 16 - 2 - H)] = jnp.zeros((16 - 2 - H, 8, 128), f32)
    scatter(T1, RR1, k2, (4, 6))

    @pl.when(me == n - 1)
    def _():
        for ref in (GF0, GF1, GF2):
            ref[pl.ds(rows, 8)] = jnp.zeros((8, H, 8, 128), f32)

    @pl.when(me < n - 1)
    def _():
        grad_copies[0].wait_recv()

    def back_filter(gf, i, slot):
        for h in range(H):

            def step(b):
                win = gf[pl.ds(b * B, B + HALO), h]
                store(slot, b, h, total(SW[i, h, j][None] * win[j : j + B] for j in range(KS)))

            loop(nb, step)

    back_filter(GF0, 0, 1)

    def mixed(h, b, x):
        a = AP[h, 1]
        earlier = AP[h, B] * x + AB[h, b]
        SA[h] = SA[h] + x * PB[h, b]
        z = RA[h] * x
        for i in range(B):
            t = b * B + (B - 1 - i)
            g = G[t, h] + jnp.sum(z, axis=0)
            if i + 1 < B:
                z = a * z
            GF1[t, h] = g * F2[t, h]
            GF2[t, h] = g * F1[t, h]
        return earlier

    reduced = []
    for h in range(H):
        arrived(A0.at[pl.ds(h * M, M)], 4 + h)
        lax.fori_loop(
            0, nb, lambda i, x: mixed(h, nb - 1 - i, x), A0[pl.ds(h * M, M)]
        )
        if h == H - 1:

            @pl.when(me > 0)
            def _():
                grad_copies[1].start()
                grad_copies[2].start()

        mine = T2.at[h]
        mine[pl.ds(0, M)] = -RT[h] * SA[h]
        filter_sums(h, KX, GF1, mine, 16)
        filter_sums(h, VX, GF2, mine, 24)
        scatter(mine, RR2.at[h], k3, (6 + h, 8 + h))

    def reduce(src, dst, size):
        dst[...] = total(src[pl.ds(i * size, size)] for i in range(n))

    arrived(RR1, 6)
    reduce(RR1, SUM1, k2)
    spread(SUM1, AG1, k2, (5, 7))

    @pl.when(me < n - 1)
    def _():
        grad_copies[1].wait_recv()
        grad_copies[2].wait_recv()

    back_filter(GF1, 1, 2)
    arrived(RR2.at[0], 8)
    reduce(RR2.at[0], SUM2.at[0], k3)
    spread(SUM2.at[0], AG2.at[0], k3, (8, 10))
    back_filter(GF2, 2, 3)
    for h in range(1, H):
        arrived(RR2.at[h], 8 + h)
        reduce(RR2.at[h], SUM2.at[h], k3)
        spread(SUM2.at[h], AG2.at[h], k3, (8 + h, 10 + h))

    for h in range(H):

        def late(b):
            at = pl.ds(b * B, B)
            gain = gainv[pl.ds(h * 8, 8), :][None]
            store(0, b, h, RS[at, h] * INVT[at] * gain)
            store(4, b, h, GS[at, h])

        loop(nb, late)

    def natural(src, at, count):
        return src[pl.ds(at, count)].reshape(count, 1024)

    arrived(AG1, 7)
    for h in range(H):
        cols = pl.ds(h * 1024, 1024)
        gr_o[:, cols] = natural(AG1, h * M, M)
        short_o[0, :, cols] = natural(AG1, 32 + h * 8, 8)[0:KS]
        gskip_o[pl.ds(h * 8, 8), :] = AG1[48 + h]
        ggain_o[pl.ds(h * 8, 8), :] = AG1[50 + h]
    for h in range(H):
        cols = pl.ds(h * 1024, 1024)
        arrived(AG2.at[h], 10 + h)
        gl_o[:, cols] = natural(AG2.at[h], 0, M)
        short_o[1, :, cols] = natural(AG2.at[h], 16, 8)[0:KS]
        short_o[2, :, cols] = natural(AG2.at[h], 24, 8)[0:KS]

    for at, dst, size in (
        (0, R1, k1), (1, X0, k1), (2, R2, k1), (3, A0, k1), (4, RR1, k2), (5, AG1, k2),
        (6, RR2.at[0], k3), (7, RR2.at[1], k3), (8, AG2.at[0], k3), (9, AG2.at[1], k3),
    ):
        sent(dst, size, at)
    others = tpr.at[pl.ds(0, ntp - 1)]
    pltpu.make_async_copy(others, others, ssem.at[10]).wait()

    @pl.when(me < n - 1)
    def _():
        for copy in halo_copies:
            copy.wait_send()

    @pl.when(me > 0)
    def _():
        for copy in grad_copies:
            copy.wait_send()


def deliver(*refs):
    ins, outs, sem = refs[:10], refs[10:20], refs[20]
    copies = [pltpu.make_async_copy(s, d, sem.at[i]) for i, (s, d) in enumerate(zip(ins, outs))]
    for copy in copies:
        copy.start()
    for copy in copies:
        copy.wait()


def shards(
    n, ntp, residual, query_in, key_in, value_in, short_filter, residues, decay_rate, skip_gain,
    norm_gain, cotangent,
):
    rows, width = residual.shape
    H = width // 1024
    nb = rows // B
    tiles = H * M

    def V(*shape, dtype=f32):
        return pltpu.VMEM(shape, dtype)

    def tm(extra=0):
        return V(rows + extra, H, 8, 128)

    def tile(count):
        return V(count, 8, 128)

    k2, k3 = 64 // n, 32 // n
    scratch = (
        [V(3, 16, width, dtype=bf16)]
        + [V(3, KS, width), V(M, width), V(M, width), V(H * 8, 128), V(H * 8, 128)]
        + [tm(8)] * 3 + [tm()] * 10 + [tm(8)] * 3
        + [V(H, B + 1, M, 8, 128)] * 2
        + [V(H, B + 1, 8, 128), V(H, M, 8, 128), V(H, M, 8, 128), V(3, H, 8, 8, 128), tile(tiles)]
        + [V(H, nb, M, 8, 128)] * 3
        + [tile(tiles)] * 8
        + [V(B, 128), V(ntp, B, 128), tile(rows), tile(rows)]
        + [V(H, M, 8, 128)] * 3
        + [V(H, B, 8, 128), V(8, 1024)]
        + [tile(64), tile(64), tile(k2), tile(64)]
        + [V(H, 32, 8, 128), V(H, 32, 8, 128), V(H, k3, 8, 128), V(H, 32, 8, 128)]
        + [pltpu.SemaphoreType.DMA((c,)) for c in (10, 11, 13, 6, 6)]
    )
    big = jax.ShapeDtypeStruct((rows, width), bf16)
    vec = jax.ShapeDtypeStruct((H * 8, 128), f32)
    out_shape = (
        [big] * 5
        + [jax.ShapeDtypeStruct((3, KS, width), f32)]
        + [jax.ShapeDtypeStruct((M, width), f32)] * 2
        + [vec, vec]
    )
    anywhere = pl.BlockSpec(memory_space=pl.ANY)
    outs = pl.pallas_call(
        functools.partial(kernel, n, ntp, rows, width),
        out_shape=[V(*o.shape, dtype=o.dtype) for o in out_shape],
        in_specs=[anywhere] * 10,
        out_specs=[pl.BlockSpec(memory_space=pltpu.VMEM)] * 10,
        scratch_shapes=scratch,
        compiler_params=pltpu.CompilerParams(
            collective_id=0, has_side_effects=True, vmem_limit_bytes=52 << 20
        ),
    )(
        residual, query_in, key_in, value_in, short_filter, residues, decay_rate,
        skip_gain.reshape(H * 8, 128), norm_gain.reshape(H * 8, 128), cotangent,
    )
    outs = pl.pallas_call(
        deliver,
        out_shape=out_shape,
        in_specs=[anywhere] * 10,
        out_specs=[anywhere] * 10,
        scratch_shapes=[pltpu.SemaphoreType.DMA((10,))],
        compiler_params=pltpu.CompilerParams(vmem_limit_bytes=1 << 20),
    )(*outs)
    return (*outs[:8], outs[8].reshape(width), outs[9].reshape(width))


def solution(mesh):
    act, par, vec = P("ctx", "tp"), P(None, "tp"), P("tp")
    short = P(None, None, "tp")
    return jax.shard_map(
        functools.partial(shards, mesh.shape["ctx"], mesh.shape["tp"]),
        mesh=mesh,
        in_specs=(act, act, act, act, short, par, par, vec, vec, act),
        out_specs=(act, act, act, act, act, short, par, par, vec, vec),
        check_vma=False,
    )
```

```python
import functools

import jax
import jax.numpy as jnp
from jax import lax
from jax.experimental import pallas as pl
from jax.experimental.pallas import tpu as pltpu
from jax.sharding import PartitionSpec as P

f32 = jnp.float32
bf16 = jnp.bfloat16
MESH = pl.DeviceIdType.MESH
B = 16
M = 16
KS = 7
HALO = KS - 1


def loop(count, step, start=0):
    def lap(i, carry):
        step(i)
        return carry

    lax.fori_loop(start, count, lap, 0)


def total(terms):
    terms = list(terms)
    while len(terms) > 1:
        terms = [
            terms[i] + terms[i + 1] if i + 1 < len(terms) else terms[i]
            for i in range(0, len(terms), 2)
        ]
    return terms[0]


def kernel(
    n, ntp, rows, width,
    res_h, q_h, k_h, v_h, sf_h, r_h, lam_h, skip_h, gain_h, cot_h,
    normed_o, gres_o, gq_o, gk_o, gv_o, short_o, gr_o, gl_o, gskip_o, ggain_o,
    halo, sfv, rv, lv, skipv, gainv,
    QX, KX, VX, RS, CT, F0, F1, F2, U, Y, DZ, GS, G, GF0, GF1, GF2,
    AP, WP, KT, RT, LM, SW, AT, XB, PB, AB,
    S1, R1, E1, X0, S2, R2, E2, A0,
    sums, tpr, NS, INVR, CFR, RA, SA, QA, CK, SG,
    T1, RR1, SUM1, AG1, T2, RR2, SUM2, AG2,
    insem, ssem, rsem, hssem, hrsem,
):
    H = width // 1024
    nb = rows // B
    D = width * ntp
    me = lax.axis_index("ctx")
    mt = lax.axis_index("tp")
    tiles = H * M
    k1 = tiles // n
    k2 = 64 // n
    k3 = 32 // n

    def peer(p):
        return (p, mt)

    nat = (normed_o, gq_o, gk_o, gv_o, gres_o)

    ins = [
        (lam_h, lv), (sf_h, sfv), (k_h, nat[2]), (v_h, nat[3]), (r_h, rv), (skip_h, skipv),
        (gain_h, gainv), (q_h, nat[1]), (res_h, nat[0]), (cot_h, nat[4]),
    ]
    in_copies = [pltpu.make_async_copy(s, d, insem.at[i]) for i, (s, d) in enumerate(ins)]
    for copy in in_copies:
        copy.start()

    barrier = pltpu.get_barrier_semaphore()

    for i in range(1, n):
        pl.semaphore_signal(
            barrier, inc=1, device_id=peer(lax.rem(me + i, n)), device_id_type=MESH
        )
    for i in range(1, ntp):
        pl.semaphore_signal(
            barrier, inc=1, device_id=(me, lax.rem(mt + i, ntp)), device_id_type=MESH
        )

    in_copies[0].wait()
    in_copies[1].wait()
    for h in range(H):
        cols = pl.ds(h * 1024, 1024)
        lam = lv[:, cols].reshape(M, 8, 128)
        AP[h, 1] = jnp.exp(-lam)
        AP[h, B] = jnp.exp(lam * (-float(B)))
        LM[h] = lam
        AT[pl.ds(h * M, M)] = jnp.exp(lam * (-float(rows)))
        for i in range(3):
            SG[0:8, :] = jnp.zeros((8, 1024), f32)
            SG[0:KS, :] = sfv[i, :, cols]
            SW[i, h] = SG[0:8, :].reshape(8, 8, 128)

    def to_tm(slot, dst, off):
        def step(i):
            v = nat[slot][pl.ds(pl.multiple_of(i * 16, 16), 16), :].astype(f32)
            dst[pl.ds(off + i * 16, 16)] = v.reshape(16, H, 8, 128)

        loop(rows // 16, step)

    in_copies[2].wait()
    to_tm(2, KX, 8)
    in_copies[3].wait()
    to_tm(3, VX, 8)

    pl.semaphore_wait(barrier, n - 1 + ntp - 1)

    def in_halo(i, src):
        return pltpu.make_async_remote_copy(
            src_ref=src.at[pl.ds(rows - 8, 8)], dst_ref=halo.at[i],
            send_sem=hssem.at[i], recv_sem=hrsem.at[i],
            device_id=peer(lax.rem(me + 1, n)), device_id_type=MESH,
        )

    halo_copies = [in_halo(0, q_h), in_halo(1, nat[2]), in_halo(2, nat[3])]

    @pl.when(me < n - 1)
    def _():
        for i in (1, 2, 0):
            halo_copies[i].start()

    def window(src, b, h):
        return src[pl.ds(b * 8 + 2, 14), h]

    def fir(win, i, h):
        return total(SW[i, h, j][None] * win[HALO - j : HALO - j + 8] for j in range(KS))

    def feature(h, b):
        at = pl.ds(b * 8, 8)
        f1 = fir(window(KX, b, h), 1, h)
        F1[at, h] = f1
        f2 = fir(window(VX, b, h), 2, h)
        F2[at, h] = f2
        U[at, h] = f1 * f2

    def gather(h, b):
        a = AP[h, 1]
        u = U[pl.ds(b * B, B), h]
        x = a * u[0][None] + u[1][None]
        for s in range(2, B):
            x = a * x + u[s][None]
        XB[h, b] = x
        return x

    def summary(h):
        def step(b, run):
            return AP[h, B] * run + gather(h, b)

        S1[pl.ds(h * M, M)] = lax.fori_loop(1, nb, step, jnp.zeros((M, 8, 128), f32))

    loop(rows // 8, functools.partial(feature, 0), 1)
    summary(0)
    for h in range(1, H):
        loop(rows // 8, functools.partial(feature, h), 1)

    def first_rows(i, dst):
        @pl.when(me > 0)
        def _():
            halo_copies[i].wait_recv()

        @pl.when(me == 0)
        def _():
            halo[i] = jnp.zeros(halo.shape[1:], bf16)

        dst[pl.ds(0, 8)] = halo[i].astype(f32).reshape(8, H, 8, 128)

    first_rows(1, KX)
    first_rows(2, VX)

    half = n // H

    def remote(src, dst, p, at):
        pltpu.make_async_remote_copy(
            src_ref=src, dst_ref=dst, send_sem=ssem.at[at[0]], recv_sem=rsem.at[at[1]],
            device_id=peer(p), device_id_type=MESH,
        ).start()

    def part(ref, p, size):
        return ref.at[pl.ds(p * size, size)]

    def scatter(src, dst, size, at):
        mine = part(dst, me, size)
        def step(i):
            p = lax.rem(me + i, n)
            remote(part(src, p, size), mine, p, at)

        loop(n, step, 1)
        pltpu.make_async_copy(part(src, me, size), mine, rsem.at[at[1]]).start()

    def scatter_half(src, dst, size, at, h):
        mine = part(dst, me, size)
        def step(i):
            p = h * half + lax.rem(me + i, half)
            remote(part(src, p, size), mine, p, at)

        loop(half, step, 1)
        first = me < half if h == 0 else me >= half
        other = me >= half if h == 0 else me < half

        @pl.when(first)
        def _():
            pltpu.make_async_copy(part(src, me, size), mine, rsem.at[at[1]]).start()

        @pl.when(other)
        def _():
            p = h * half + lax.rem(me, half)
            remote(part(src, p, size), mine, p, at)

    def spread(src, dst, size, at):
        mine = part(dst, me, size)
        loop(n, lambda i: remote(src, mine, lax.rem(me + i, n), at), 1)
        pltpu.make_async_copy(src, mine, rsem.at[at[1]]).start()

    def arrived(dst, at):
        pltpu.make_async_copy(dst, dst, rsem.at[at]).wait()

    def sent(dst, size, at):
        all_but_one = dst.at[pl.ds(0, (n - 1) * size)]
        pltpu.make_async_copy(all_but_one, all_but_one, ssem.at[at]).wait()

    def scan(src, dst, backward):
        a = AT[pl.ds(me * k1, k1)]
        run = jnp.zeros((k1, 8, 128), f32)
        for i in range(n):
            d = n - 1 - i if backward else i
            at = pl.ds(d * k1, k1)
            dst[at] = run
            run = a * run + src[at]

    def relay(src, mid, dst, at, backward, h):
        @pl.when(me < half if h == 0 else me >= half)
        def _():
            arrived(src, at[1])
            scan(src, mid, backward)
            scatter(mid, dst, k1, (at[0] + 1, at[1] + 1 + h))

    for h in range(H):
        if h > 0:
            summary(h)
        feature(h, 0)
        S1[pl.ds(h * M, M)] = S1[pl.ds(h * M, M)] + gather(h, 0) * jnp.exp(
            LM[h] * (-float(rows - B))
        )
        scatter_half(S1, R1, k1, (0, 0), h)

    for i in (4, 5, 6):
        in_copies[i].wait()
    for h in range(H):
        r = rv[:, pl.ds(h * 1024, 1024)].reshape(M, 8, 128)
        RT[h] = r

        def powers(k):
            p = jnp.exp(LM[h] * (-k.astype(f32)))
            AP[h, k] = p
            WP[h, k] = p * k.astype(f32)
            KT[h, k] = jnp.sum(r * p, axis=0)

        loop(B + 1, powers)
        KT[h, 0] = KT[h, 0] + skipv[pl.ds(h * 8, 8), :]
        RA[h] = r * AP[h, 1]

    def inside(h):
        def step(b):
            u = [U[b * B + t, h] for t in range(B)]
            kt = [KT[h, k] for k in range(B)]
            for t in range(B):
                Y[b * B + t, h] = total(kt[k] * u[t - k] for k in range(t + 1))

        loop(nb, step)

    loop(H, inside)
    in_copies[7].wait()
    to_tm(1, QX, 8)
    first_rows(0, QX)
    relay(R1, E1, X0, (0, 0), False, 0)
    relay(R1, E1, X0, (0, 0), False, 1)

    def feature_q(h):
        def step(b):
            F0[pl.ds(b * 8, 8), h] = fir(window(QX, b, h), 0, h)

        loop(rows // 8, step)

    loop(H, feature_q)
    in_copies[8].wait()
    to_tm(0, RS, 0)
    in_copies[9].wait()
    gain_tm = gainv[...].reshape(1, H, 8, 128)

    def to_gain_term(i):
        v = nat[4][pl.ds(pl.multiple_of(i * 16, 16), 16), :].astype(f32)
        CT[pl.ds(i * 16, 16)] = v.reshape(16, H, 8, 128) * gain_tm

    loop(rows // 16, to_gain_term)

    def total_in_order(terms):
        out = terms[0]
        for term in terms[1:]:
            out = out + term
        return out

    def weighted(h):
        edge = (float(B) * AP[h, 1]) * AP[h, B]

        def step(b):
            u = U[pl.ds(b * B, B), h]
            PB[h, b] = total_in_order(
                [edge * XB[h, b]] + [WP[h, B - s] * u[s][None] for s in range(B)]
            )

        loop(nb, step)

    groups = rows // 8
    lane = lax.broadcasted_iota(jnp.int32, (8, 128), 1)

    def fold(parts):
        flat = jnp.stack(parts).reshape(8, 1024)
        return total(flat[:, i * 128 : (i + 1) * 128] for i in range(8))

    def forward(h, b, x):
        a = AP[h, 1]
        z = RA[h] * x
        later = AP[h, B] * x + XB[h, b]
        XB[h, b] = x
        squares, inner = [], []
        for i in range(B):
            t = b * B + i
            y = Y[t, h] + jnp.sum(z, axis=0)
            if i + 1 < B:
                z = a * z
            Y[t, h] = y
            s = RS[t, h] + F0[t, h] * y
            RS[t, h] = s
            squares.append(s * s)
            inner.append(CT[t, h] * s)
            if h > 0:
                squares[i] = squares[i] + G[t, 0]
                inner[i] = inner[i] + GS[t, 0]
            if h < H - 1:
                G[t, 0] = squares[i]
                GS[t, 0] = inner[i]
            if h == H - 1 and i % 8 == 7:
                NS[0, b * 2 + i // 8] = fold(squares[i - 7 : i + 1])
                NS[1, b * 2 + i // 8] = fold(inner[i - 7 : i + 1])
        return later

    for h in range(H):
        arrived(X0.at[pl.ds(h * M, M)], 1 + h)
        lax.fori_loop(0, nb, functools.partial(forward, h), X0[pl.ds(h * M, M)])
    gathered = jnp.zeros((8, 128), f32)
    for q in range(2):
        for g in range(groups):
            col = jnp.sum(NS[q, g], axis=1, keepdims=True)
            gathered = jnp.where(lane == q * groups + g, col, gathered)
    sums[...] = gathered
    for i in range(1, ntp):
        p = lax.rem(mt + i, ntp)
        pltpu.make_async_remote_copy(
            src_ref=sums, dst_ref=tpr.at[mt], send_sem=ssem.at[10], recv_sem=rsem.at[12],
            device_id=(me, p), device_id_type=MESH,
        ).start()
    pltpu.make_async_copy(sums, tpr.at[mt], rsem.at[12]).start()
    loop(H, weighted)
    arrived(tpr, 12)
    tot = total(tpr[i] for i in range(ntp))
    inner_sum = pltpu.roll(tot, 128 - groups, 1)
    valid = lane < groups
    inv_all = lax.rsqrt(jnp.where(valid, tot, 1.0) / D + 1e-5)
    coef_all = inv_all * inv_all * inv_all * jnp.where(valid, inner_sum, 0.0) / D

    for g in range(groups):
        at = pl.ds(g * 8, 8)
        INVR[at, :] = jnp.broadcast_to(inv_all[:, g : g + 1], (8, 128))
        CFR[at, :] = jnp.broadcast_to(coef_all[:, g : g + 1], (8, 128))

    def row(ref, t):
        return jnp.broadcast_to(ref[pl.ds(t, 1), :], (8, 128))

    def backward(h):
        a = AP[h, 1]

        def step(i, run):
            b = nb - 1 - i
            at = pl.ds(b * B, B)
            inv = jnp.stack([row(INVR, b * B + t) for t in range(B)])
            coef = jnp.stack([row(CFR, b * B + t) for t in range(B)])
            gs = inv * CT[at, h] - RS[at, h] * coef
            GS[at, h] = gs
            dz = gs * F0[at, h]
            DZ[at, h] = dz
            v = a * dz[B - 1][None] + dz[B - 2][None]
            for s in range(B - 3, -1, -1):
                v = a * v + dz[s][None]
            AB[h, b] = v
            return AP[h, B] * run + v

        S2[pl.ds(h * M, M)] = lax.fori_loop(0, nb, step, jnp.zeros((M, 8, 128), f32))

    for h in range(H):
        backward(h)
        scatter_half(S2, R2, k1, (2, 3), h)

    def store(slot, b, h, value):
        nat[slot][pl.ds(pl.multiple_of(b * 16, 16), 16), pl.ds(h * 1024, 1024)] = value.reshape(
            B, 1024
        ).astype(bf16)

    for h in range(H):

        def early(b, acc):
            at = pl.ds(b * B, B)
            GF0[at, h] = GS[at, h] * Y[at, h]
            inv = jnp.stack([row(INVR, b * B + t) for t in range(B)])
            return acc + jnp.sum(CT[at, h] * (RS[at, h] * inv), axis=0)

        acc = lax.fori_loop(0, nb, early, jnp.zeros((8, 128), f32))
        T1[50 + h] = acc / gainv[pl.ds(h * 8, 8), :]

    def grad_halo(i, ref):
        return pltpu.make_async_remote_copy(
            src_ref=ref.at[pl.ds(0, HALO)], dst_ref=ref.at[pl.ds(rows, HALO)],
            send_sem=hssem.at[3 + i], recv_sem=hrsem.at[3 + i],
            device_id=peer(lax.rem(me + n - 1, n)), device_id_type=MESH,
        )

    grad_copies = [grad_halo(i, ref) for i, ref in enumerate((GF0, GF1, GF2))]

    @pl.when(me > 0)
    def _():
        grad_copies[0].start()

    def correlate(h):
        def step(b, acc):
            u = [U[b * B + t, h] for t in range(B)]
            dz = [DZ[b * B + t, h] for t in range(B)]
            return tuple(
                acc[k] + total(dz[t] * u[t - k] for t in range(k, B)) for k in range(B)
            )

        zero = jnp.zeros((8, 128), f32)
        out = lax.fori_loop(0, nb, step, (zero,) * B)
        for k in range(B):
            CK[h, k] = out[k]

    loop(H, correlate)

    def filter_sums(h, src, gf, dst, base):
        def step(b, acc):
            win = window(src, b, h)
            g = gf[pl.ds(b * 8, 8), h]
            return tuple(
                acc[j] + jnp.sum(g * win[HALO - j : HALO - j + 8], axis=0) for j in range(KS)
            )

        zero = jnp.zeros((8, 128), f32)
        out = lax.fori_loop(0, rows // 8, step, (zero,) * KS)
        for j in range(KS):
            dst[base + j] = out[j]
        dst[base + KS] = zero

    for h in range(H):
        filter_sums(h, QX, GF0, T1, 32 + h * 8)
    T1[pl.ds(48 + 2 + H, 16 - 2 - H)] = jnp.zeros((16 - 2 - H, 8, 128), f32)

    def inside_back(h):
        def step(b):
            dz = [DZ[b * B + t, h] for t in range(B)]
            kt = [KT[h, k] for k in range(B)]
            for s in range(B):
                G[b * B + s, h] = total(kt[k] * dz[s + k] for k in range(B - s))

        loop(nb, step)


    def mode_sums(h):
        def step(b):
            dz = DZ[pl.ds(b * B, B), h]
            x = XB[h, b]
            QA[h] = QA[h] + x * AB[h, b]
            q = total_in_order([WP[h, s] * dz[s][None] for s in range(1, B)])
            SA[h] = SA[h] + x * q

        QA[h] = jnp.zeros((M, 8, 128), f32)
        SA[h] = jnp.zeros((M, 8, 128), f32)
        loop(nb, step)
        a = AP[h, 1]
        gr = a * QA[h]
        gl = a * SA[h]
        for k in range(B):
            c = CK[h, k][None]
            gr = gr + AP[h, k] * c
            gl = gl + WP[h, k] * c
        T1[pl.ds(h * M, M)] = gr
        SA[h] = gl
        T1[48 + h] = CK[h, 0]

    mode_sums(0)
    relay(R2, E2, A0, (2, 3), True, 0)
    loop(H, mode_sums, 1)
    relay(R2, E2, A0, (2, 3), True, 1)
    loop(H, inside_back)

    @pl.when(me == n - 1)
    def _():
        for ref in (GF0, GF1, GF2):
            ref[pl.ds(rows, 8)] = jnp.zeros((8, H, 8, 128), f32)

    @pl.when(me < n - 1)
    def _():
        grad_copies[0].wait_recv()

    def back_filter(gf, i, slot):
        for h in range(H):

            def step(b):
                win = gf[pl.ds(b * B, B + HALO), h]
                store(slot, b, h, total(SW[i, h, j][None] * win[j : j + B] for j in range(KS)))

            loop(nb, step)

    @pl.when(me < n - 1)
    def _():
        for copy in halo_copies:
            copy.wait_send()

    back_filter(GF0, 0, 1)

    def mixed(h, b, x):
        a = AP[h, 1]
        earlier = AP[h, B] * x + AB[h, b]
        SA[h] = SA[h] + x * PB[h, b]
        z = RA[h] * x
        for i in range(B):
            t = b * B + (B - 1 - i)
            g = G[t, h] + jnp.sum(z, axis=0)
            if i + 1 < B:
                z = a * z
            GF1[t, h] = g * F2[t, h]
            GF2[t, h] = g * F1[t, h]
        return earlier

    def reduce(src, dst, size):
        dst[...] = total(src[pl.ds(i * size, size)] for i in range(n))

    for h in range(H):
        arrived(A0.at[pl.ds(h * M, M)], 4 + h)
        if h == 0:
            scatter(T1, RR1, k2, (4, 6))
        lax.fori_loop(
            0, nb, lambda i, x: mixed(h, nb - 1 - i, x), A0[pl.ds(h * M, M)]
        )
        if h == H - 1:

            @pl.when(me > 0)
            def _():
                grad_copies[1].start()
                grad_copies[2].start()

        mine = T2.at[h]
        mine[pl.ds(0, M)] = -RT[h] * SA[h]
        filter_sums(h, KX, GF1, mine, 16)
        filter_sums(h, VX, GF2, mine, 24)
        scatter(mine, RR2.at[h], k3, (6 + h, 8 + h))

    @pl.when(me < n - 1)
    def _():
        grad_copies[1].wait_recv()
        grad_copies[2].wait_recv()

    back_filter(GF1, 1, 2)
    arrived(RR1, 6)
    reduce(RR1, SUM1, k2)
    spread(SUM1, AG1, k2, (5, 7))
    arrived(RR2.at[0], 8)
    reduce(RR2.at[0], SUM2.at[0], k3)
    spread(SUM2.at[0], AG2.at[0], k3, (8, 10))
    back_filter(GF2, 2, 3)
    for h in range(1, H):
        arrived(RR2.at[h], 8 + h)
        reduce(RR2.at[h], SUM2.at[h], k3)
        spread(SUM2.at[h], AG2.at[h], k3, (8 + h, 10 + h))

    for h in range(H):

        def late(b):
            at = pl.ds(b * B, B)
            gain = gainv[pl.ds(h * 8, 8), :][None]
            inv = jnp.stack([row(INVR, b * B + t) for t in range(B)])
            store(0, b, h, RS[at, h] * inv * gain)
            store(4, b, h, GS[at, h])

        loop(nb, late)

    def natural(src, at, count):
        return src[pl.ds(at, count)].reshape(count, 1024)

    arrived(AG1, 7)
    for h in range(H):
        cols = pl.ds(h * 1024, 1024)
        gr_o[:, cols] = natural(AG1, h * M, M)
        short_o[0, :, cols] = natural(AG1, 32 + h * 8, 8)[0:KS]
        gskip_o[pl.ds(h * 8, 8), :] = AG1[48 + h]
        ggain_o[pl.ds(h * 8, 8), :] = AG1[50 + h]
    for h in range(H):
        cols = pl.ds(h * 1024, 1024)
        arrived(AG2.at[h], 10 + h)
        gl_o[:, cols] = natural(AG2.at[h], 0, M)
        short_o[1, :, cols] = natural(AG2.at[h], 16, 8)[0:KS]
        short_o[2, :, cols] = natural(AG2.at[h], 24, 8)[0:KS]

    for at, dst, size in (
        (0, R1, k1), (1, X0, k1), (2, R2, k1), (3, A0, k1), (4, RR1, k2), (5, AG1, k2),
        (6, RR2.at[0], k3), (7, RR2.at[1], k3), (8, AG2.at[0], k3), (9, AG2.at[1], k3),
    ):
        sent(dst, size, at)
    others = tpr.at[pl.ds(0, ntp - 1)]
    pltpu.make_async_copy(others, others, ssem.at[10]).wait()

    @pl.when(me > 0)
    def _():
        for copy in grad_copies:
            copy.wait_send()


def deliver(*refs):
    ins, outs, sem = refs[:10], refs[10:20], refs[20]
    copies = [pltpu.make_async_copy(s, d, sem.at[i]) for i, (s, d) in enumerate(zip(ins, outs))]
    for copy in copies:
        copy.start()
    for copy in copies:
        copy.wait()


def shards(
    n, ntp, residual, query_in, key_in, value_in, short_filter, residues, decay_rate, skip_gain,
    norm_gain, cotangent,
):
    rows, width = residual.shape
    H = width // 1024
    nb = rows // B
    tiles = H * M

    def V(*shape, dtype=f32):
        return pltpu.VMEM(shape, dtype)

    def tm(extra=0):
        return V(rows + extra, H, 8, 128)

    def tile(count):
        return V(count, 8, 128)

    k2, k3 = 64 // n, 32 // n
    scratch = (
        [V(3, 8, width, dtype=bf16)]
        + [V(3, KS, width), V(M, width), V(M, width), V(H * 8, 128), V(H * 8, 128)]
        + [tm(8)] * 3 + [tm()] * 10 + [tm(8)] * 3
        + [V(H, B + 1, M, 8, 128)] * 2
        + [V(H, B + 1, 8, 128), V(H, M, 8, 128), V(H, M, 8, 128), V(3, H, 8, 8, 128), tile(tiles)]
        + [V(H, nb, M, 8, 128)] * 3
        + [tile(tiles)] * 8
        + [V(8, 128), tile(ntp), V(2, rows // 8, 8, 128), V(rows, 128), V(rows, 128)]
        + [V(H, M, 8, 128)] * 3
        + [V(H, B, 8, 128), V(8, 1024)]
        + [tile(64), tile(64), tile(k2), tile(64)]
        + [V(H, 32, 8, 128), V(H, 32, 8, 128), V(H, k3, 8, 128), V(H, 32, 8, 128)]
        + [pltpu.SemaphoreType.DMA((c,)) for c in (10, 11, 13, 6, 6)]
    )
    big = jax.ShapeDtypeStruct((rows, width), bf16)
    vec = jax.ShapeDtypeStruct((H * 8, 128), f32)
    out_shape = (
        [big] * 5
        + [jax.ShapeDtypeStruct((3, KS, width), f32)]
        + [jax.ShapeDtypeStruct((M, width), f32)] * 2
        + [vec, vec]
    )
    anywhere = pl.BlockSpec(memory_space=pl.ANY)
    outs = pl.pallas_call(
        functools.partial(kernel, n, ntp, rows, width),
        out_shape=[V(*o.shape, dtype=o.dtype) for o in out_shape],
        in_specs=[anywhere] * 10,
        out_specs=[pl.BlockSpec(memory_space=pltpu.VMEM)] * 10,
        scratch_shapes=scratch,
        compiler_params=pltpu.CompilerParams(
            collective_id=0, has_side_effects=True, vmem_limit_bytes=52 << 20
        ),
    )(
        residual, query_in, key_in, value_in, short_filter, residues, decay_rate,
        skip_gain.reshape(H * 8, 128), norm_gain.reshape(H * 8, 128), cotangent,
    )
    outs = pl.pallas_call(
        deliver,
        out_shape=out_shape,
        in_specs=[anywhere] * 10,
        out_specs=[anywhere] * 10,
        scratch_shapes=[pltpu.SemaphoreType.DMA((10,))],
        compiler_params=pltpu.CompilerParams(vmem_limit_bytes=1 << 20),
    )(*outs)
    return (*outs[:8], outs[8].reshape(width), outs[9].reshape(width))


def solution(mesh):
    act, par, vec = P("ctx", "tp"), P(None, "tp"), P("tp")
    short = P(None, None, "tp")
    return jax.shard_map(
        functools.partial(shards, mesh.shape["ctx"], mesh.shape["tp"]),
        mesh=mesh,
        in_specs=(act, act, act, act, short, par, par, vec, vec, act),
        out_specs=(act, act, act, act, act, short, par, par, vec, vec),
        check_vma=False,
    )
```

```python
import functools

import jax
import jax.numpy as jnp
from jax import lax
from jax.experimental import pallas as pl
from jax.experimental.pallas import tpu as pltpu
from jax.sharding import PartitionSpec as P

f32 = jnp.float32
bf16 = jnp.bfloat16
MESH = pl.DeviceIdType.MESH
B = 16
M = 16
KS = 7
HALO = KS - 1


def loop(count, step, start=0):
    def lap(i, carry):
        step(i)
        return carry

    lax.fori_loop(start, count, lap, 0)


def total(terms):
    terms = list(terms)
    while len(terms) > 1:
        terms = [
            terms[i] + terms[i + 1] if i + 1 < len(terms) else terms[i]
            for i in range(0, len(terms), 2)
        ]
    return terms[0]


def kernel(
    n, ntp, rows, width,
    res_h, q_h, k_h, v_h, sf_h, r_h, lam_h, skip_h, gain_h, cot_h,
    normed_o, gres_o, gq_o, gk_o, gv_o, short_o, gr_o, gl_o, gskip_o, ggain_o,
    halo, sfv, rv, lv, skipv, gainv,
    QX, KX, VX, RS, CT, F0, F1, F2, U, Y, DZ, GS, G, GF0, GF1, GF2,
    AP, WP, KT, RT, LM, SW, AT, XB, PB, AB,
    S1, R1, E1, X0, S2, R2, E2, A0,
    sums, tpr, NS, INVR, CFR, RA, SA, QA, CK, SG,
    T1, RR1, SUM1, AG1, T1A, RR1A, SUM1A, AG1A, T2, RR2, SUM2, AG2,
    insem, ssem, rsem, hssem, hrsem,
):
    H = width // 1024
    nb = rows // B
    D = width * ntp
    me = lax.axis_index("ctx")
    mt = lax.axis_index("tp")
    tiles = H * M
    k1 = tiles // n
    k3 = 32 // n

    def peer(p):
        return (p, mt)

    nat = (normed_o, gq_o, gk_o, gv_o, gres_o)

    ins = [
        (lam_h, lv), (sf_h, sfv), (k_h, nat[2]), (v_h, nat[3]), (r_h, rv), (skip_h, skipv),
        (gain_h, gainv), (q_h, nat[1]), (res_h, nat[0]), (cot_h, nat[4]),
    ]
    in_copies = [pltpu.make_async_copy(s, d, insem.at[i]) for i, (s, d) in enumerate(ins)]
    for copy in in_copies:
        copy.start()

    barrier = pltpu.get_barrier_semaphore()

    for i in range(1, n):
        pl.semaphore_signal(
            barrier, inc=1, device_id=peer(lax.rem(me + i, n)), device_id_type=MESH
        )
    for i in range(1, ntp):
        pl.semaphore_signal(
            barrier, inc=1, device_id=(me, lax.rem(mt + i, ntp)), device_id_type=MESH
        )

    in_copies[0].wait()
    in_copies[1].wait()
    for h in range(H):
        cols = pl.ds(h * 1024, 1024)
        lam = lv[:, cols].reshape(M, 8, 128)
        AP[h, 1] = jnp.exp(-lam)
        AP[h, B] = jnp.exp(lam * (-float(B)))
        LM[h] = lam
        AT[pl.ds(h * M, M)] = jnp.exp(lam * (-float(rows)))
        for i in range(3):
            SG[0:8, :] = jnp.zeros((8, 1024), f32)
            SG[0:KS, :] = sfv[i, :, cols]
            SW[i, h] = SG[0:8, :].reshape(8, 8, 128)

    def to_tm(slot, dst, off):
        def step(i):
            v = nat[slot][pl.ds(pl.multiple_of(i * 16, 16), 16), :].astype(f32)
            dst[pl.ds(off + i * 16, 16)] = v.reshape(16, H, 8, 128)

        loop(rows // 16, step)

    in_copies[2].wait()
    to_tm(2, KX, 8)
    in_copies[3].wait()
    to_tm(3, VX, 8)

    pl.semaphore_wait(barrier, n - 1 + ntp - 1)

    def in_halo(i, src):
        return pltpu.make_async_remote_copy(
            src_ref=src.at[pl.ds(rows - 8, 8)], dst_ref=halo.at[i],
            send_sem=hssem.at[i], recv_sem=hrsem.at[i],
            device_id=peer(lax.rem(me + 1, n)), device_id_type=MESH,
        )

    halo_copies = [in_halo(0, q_h), in_halo(1, nat[2]), in_halo(2, nat[3])]

    @pl.when(me < n - 1)
    def _():
        for i in (1, 2, 0):
            halo_copies[i].start()

    def window(src, b, h):
        return src[pl.ds(b * 8 + 2, 14), h]

    def fir(win, i, h):
        return total(SW[i, h, j][None] * win[HALO - j : HALO - j + 8] for j in range(KS))

    def feature(h, b):
        at = pl.ds(b * 8, 8)
        f1 = fir(window(KX, b, h), 1, h)
        F1[at, h] = f1
        f2 = fir(window(VX, b, h), 2, h)
        F2[at, h] = f2
        U[at, h] = f1 * f2

    def gather(h, b):
        a = AP[h, 1]
        u = U[pl.ds(b * B, B), h]
        x = a * u[0][None] + u[1][None]
        for s in range(2, B):
            x = a * x + u[s][None]
        XB[h, b] = x
        return x

    def summary(h):
        def step(b, run):
            return AP[h, B] * run + gather(h, b)

        S1[pl.ds(h * M, M)] = lax.fori_loop(1, nb, step, jnp.zeros((M, 8, 128), f32))

    loop(rows // 8, functools.partial(feature, 0), 1)
    summary(0)
    for h in range(1, H):
        loop(rows // 8, functools.partial(feature, h), 1)

    def first_rows(i, dst):
        @pl.when(me > 0)
        def _():
            halo_copies[i].wait_recv()

        @pl.when(me == 0)
        def _():
            halo[i] = jnp.zeros(halo.shape[1:], bf16)

        dst[pl.ds(0, 8)] = halo[i].astype(f32).reshape(8, H, 8, 128)

    first_rows(1, KX)
    first_rows(2, VX)

    half = n // H

    def remote(src, dst, p, at):
        pltpu.make_async_remote_copy(
            src_ref=src, dst_ref=dst, send_sem=ssem.at[at[0]], recv_sem=rsem.at[at[1]],
            device_id=peer(p), device_id_type=MESH,
        ).start()

    def part(ref, p, size):
        return ref.at[pl.ds(p * size, size)]

    def scatter(src, dst, size, at):
        mine = part(dst, me, size)
        def step(i):
            p = lax.rem(me + i, n)
            remote(part(src, p, size), mine, p, at)

        loop(n, step, 1)
        pltpu.make_async_copy(part(src, me, size), mine, rsem.at[at[1]]).start()

    def scatter_half(src, dst, size, at, h):
        mine = part(dst, me, size)
        def step(i):
            p = h * half + lax.rem(me + i, half)
            remote(part(src, p, size), mine, p, at)

        loop(half, step, 1)
        first = me < half if h == 0 else me >= half
        other = me >= half if h == 0 else me < half

        @pl.when(first)
        def _():
            pltpu.make_async_copy(part(src, me, size), mine, rsem.at[at[1]]).start()

        @pl.when(other)
        def _():
            p = h * half + lax.rem(me, half)
            remote(part(src, p, size), mine, p, at)

    def spread(src, dst, size, at):
        mine = part(dst, me, size)
        loop(n, lambda i: remote(src, mine, lax.rem(me + i, n), at), 1)
        pltpu.make_async_copy(src, mine, rsem.at[at[1]]).start()

    def arrived(dst, at):
        pltpu.make_async_copy(dst, dst, rsem.at[at]).wait()

    def sent(dst, size, at):
        all_but_one = dst.at[pl.ds(0, (n - 1) * size)]
        pltpu.make_async_copy(all_but_one, all_but_one, ssem.at[at]).wait()

    def scan(src, dst, backward):
        a = AT[pl.ds(me * k1, k1)]
        run = jnp.zeros((k1, 8, 128), f32)
        for i in range(n):
            d = n - 1 - i if backward else i
            at = pl.ds(d * k1, k1)
            dst[at] = run
            run = a * run + src[at]

    def relay(src, mid, dst, at, backward, h):
        @pl.when(me < half if h == 0 else me >= half)
        def _():
            arrived(src, at[1])
            scan(src, mid, backward)
            scatter(mid, dst, k1, (at[0] + 1, at[1] + 1 + h))

    for h in range(H):
        if h > 0:
            summary(h)
        feature(h, 0)
        S1[pl.ds(h * M, M)] = S1[pl.ds(h * M, M)] + gather(h, 0) * jnp.exp(
            LM[h] * (-float(rows - B))
        )
        scatter_half(S1, R1, k1, (0, 0), h)

    for i in (4, 5, 6):
        in_copies[i].wait()
    for h in range(H):
        r = rv[:, pl.ds(h * 1024, 1024)].reshape(M, 8, 128)
        RT[h] = r

        def powers(k):
            p = jnp.exp(LM[h] * (-k.astype(f32)))
            AP[h, k] = p
            WP[h, k] = p * k.astype(f32)
            KT[h, k] = jnp.sum(r * p, axis=0)

        loop(B + 1, powers)
        KT[h, 0] = KT[h, 0] + skipv[pl.ds(h * 8, 8), :]
        RA[h] = r * AP[h, 1]

    def inside(h):
        def step(b):
            u = [U[b * B + t, h] for t in range(B)]
            kt = [KT[h, k] for k in range(B)]
            for t in range(B):
                Y[b * B + t, h] = total(kt[k] * u[t - k] for k in range(t + 1))

        loop(nb, step)

    loop(H, inside)
    in_copies[7].wait()
    to_tm(1, QX, 8)
    first_rows(0, QX)
    relay(R1, E1, X0, (0, 0), False, 0)
    relay(R1, E1, X0, (0, 0), False, 1)

    def feature_q(h):
        def step(b):
            F0[pl.ds(b * 8, 8), h] = fir(window(QX, b, h), 0, h)

        loop(rows // 8, step)

    loop(H, feature_q)
    in_copies[8].wait()
    to_tm(0, RS, 0)
    in_copies[9].wait()
    gain_tm = gainv[...].reshape(1, H, 8, 128)

    def to_gain_term(i):
        v = nat[4][pl.ds(pl.multiple_of(i * 16, 16), 16), :].astype(f32)
        CT[pl.ds(i * 16, 16)] = v.reshape(16, H, 8, 128) * gain_tm

    loop(rows // 16, to_gain_term)

    def total_in_order(terms):
        out = terms[0]
        for term in terms[1:]:
            out = out + term
        return out

    def weighted(h):
        edge = (float(B) * AP[h, 1]) * AP[h, B]

        def step(b):
            u = U[pl.ds(b * B, B), h]
            PB[h, b] = total_in_order(
                [edge * XB[h, b]] + [WP[h, B - s] * u[s][None] for s in range(B)]
            )

        loop(nb, step)

    groups = rows // 8
    lane = lax.broadcasted_iota(jnp.int32, (8, 128), 1)

    def fold(parts):
        flat = jnp.stack(parts).reshape(8, 1024)
        return total(flat[:, i * 128 : (i + 1) * 128] for i in range(8))

    def forward(h, b, x):
        a = AP[h, 1]
        z = RA[h] * x
        later = AP[h, B] * x + XB[h, b]
        XB[h, b] = x
        squares, inner = [], []
        for i in range(B):
            t = b * B + i
            y = Y[t, h] + jnp.sum(z, axis=0)
            if i + 1 < B:
                z = a * z
            Y[t, h] = y
            s = RS[t, h] + F0[t, h] * y
            RS[t, h] = s
            squares.append(s * s)
            inner.append(CT[t, h] * s)
            if h > 0:
                squares[i] = squares[i] + G[t, 0]
                inner[i] = inner[i] + GS[t, 0]
            if h < H - 1:
                G[t, 0] = squares[i]
                GS[t, 0] = inner[i]
            if h == H - 1 and i % 8 == 7:
                NS[0, b * 2 + i // 8] = fold(squares[i - 7 : i + 1])
                NS[1, b * 2 + i // 8] = fold(inner[i - 7 : i + 1])
        return later

    for h in range(H):
        arrived(X0.at[pl.ds(h * M, M)], 1 + h)
        lax.fori_loop(0, nb, functools.partial(forward, h), X0[pl.ds(h * M, M)])
    gathered = jnp.zeros((8, 128), f32)
    for q in range(2):
        for g in range(groups):
            col = jnp.sum(NS[q, g], axis=1, keepdims=True)
            gathered = jnp.where(lane == q * groups + g, col, gathered)
    sums[...] = gathered
    for i in range(1, ntp):
        p = lax.rem(mt + i, ntp)
        pltpu.make_async_remote_copy(
            src_ref=sums, dst_ref=tpr.at[mt], send_sem=ssem.at[10], recv_sem=rsem.at[12],
            device_id=(me, p), device_id_type=MESH,
        ).start()
    pltpu.make_async_copy(sums, tpr.at[mt], rsem.at[12]).start()
    loop(H, weighted)
    arrived(tpr, 12)
    tot = total(tpr[i] for i in range(ntp))
    inner_sum = pltpu.roll(tot, 128 - groups, 1)
    valid = lane < groups
    inv_all = lax.rsqrt(jnp.where(valid, tot, 1.0) / D + 1e-5)
    coef_all = inv_all * inv_all * inv_all * jnp.where(valid, inner_sum, 0.0) / D

    for g in range(groups):
        at = pl.ds(g * 8, 8)
        INVR[at, :] = jnp.broadcast_to(inv_all[:, g : g + 1], (8, 128))
        CFR[at, :] = jnp.broadcast_to(coef_all[:, g : g + 1], (8, 128))

    def row(ref, t):
        return jnp.broadcast_to(ref[pl.ds(t, 1), :], (8, 128))

    def backward(h):
        a = AP[h, 1]

        def step(i, run):
            b = nb - 1 - i
            at = pl.ds(b * B, B)
            inv = jnp.stack([row(INVR, b * B + t) for t in range(B)])
            coef = jnp.stack([row(CFR, b * B + t) for t in range(B)])
            gs = inv * CT[at, h] - RS[at, h] * coef
            GS[at, h] = gs
            dz = gs * F0[at, h]
            DZ[at, h] = dz
            v = a * dz[B - 1][None] + dz[B - 2][None]
            for s in range(B - 3, -1, -1):
                v = a * v + dz[s][None]
            AB[h, b] = v
            return AP[h, B] * run + v

        S2[pl.ds(h * M, M)] = lax.fori_loop(0, nb, step, jnp.zeros((M, 8, 128), f32))

    for h in range(H):
        backward(h)
        scatter_half(S2, R2, k1, (2, 3), h)

    def store(slot, b, h, value):
        nat[slot][pl.ds(pl.multiple_of(b * 16, 16), 16), pl.ds(h * 1024, 1024)] = value.reshape(
            B, 1024
        ).astype(bf16)

    for h in range(H):

        def early(b, acc):
            at = pl.ds(b * B, B)
            GF0[at, h] = GS[at, h] * Y[at, h]
            inv = jnp.stack([row(INVR, b * B + t) for t in range(B)])
            return acc + jnp.sum(CT[at, h] * (RS[at, h] * inv), axis=0)

        acc = lax.fori_loop(0, nb, early, jnp.zeros((8, 128), f32))
        T1A[18 + h] = acc / gainv[pl.ds(h * 8, 8), :]

    def grad_halo(i, ref):
        return pltpu.make_async_remote_copy(
            src_ref=ref.at[pl.ds(0, HALO)], dst_ref=ref.at[pl.ds(rows, HALO)],
            send_sem=hssem.at[3 + i], recv_sem=hrsem.at[3 + i],
            device_id=peer(lax.rem(me + n - 1, n)), device_id_type=MESH,
        )

    grad_copies = [grad_halo(i, ref) for i, ref in enumerate((GF0, GF1, GF2))]

    @pl.when(me > 0)
    def _():
        grad_copies[0].start()

    def correlate(h):
        def step(b, acc):
            u = [U[b * B + t, h] for t in range(B)]
            dz = [DZ[b * B + t, h] for t in range(B)]
            return tuple(
                acc[k] + total(dz[t] * u[t - k] for t in range(k, B)) for k in range(B)
            )

        zero = jnp.zeros((8, 128), f32)
        out = lax.fori_loop(0, nb, step, (zero,) * B)
        for k in range(B):
            CK[h, k] = out[k]

    loop(H, correlate)

    def filter_sums(h, src, gf, dst, base):
        def step(b, acc):
            win = window(src, b, h)
            g = gf[pl.ds(b * 8, 8), h]
            return tuple(
                acc[j] + jnp.sum(g * win[HALO - j : HALO - j + 8], axis=0) for j in range(KS)
            )

        zero = jnp.zeros((8, 128), f32)
        out = lax.fori_loop(0, rows // 8, step, (zero,) * KS)
        for j in range(KS):
            dst[base + j] = out[j]
        dst[base + KS] = zero

    for h in range(H):
        filter_sums(h, QX, GF0, T1A, h * 8)
        T1A[16 + h] = CK[h, 0]
    T1A[pl.ds(18 + H, 14 - H)] = jnp.zeros((14 - H, 8, 128), f32)
    scatter(T1A, RR1A, k3, (11, 13))

    def inside_back(h):
        def step(b):
            dz = [DZ[b * B + t, h] for t in range(B)]
            kt = [KT[h, k] for k in range(B)]
            for s in range(B):
                G[b * B + s, h] = total(kt[k] * dz[s + k] for k in range(B - s))

        loop(nb, step)


    def mode_sums(h):
        def step(b):
            dz = DZ[pl.ds(b * B, B), h]
            x = XB[h, b]
            QA[h] = QA[h] + x * AB[h, b]
            q = total_in_order([WP[h, s] * dz[s][None] for s in range(1, B)])
            SA[h] = SA[h] + x * q

        QA[h] = jnp.zeros((M, 8, 128), f32)
        SA[h] = jnp.zeros((M, 8, 128), f32)
        loop(nb, step)
        a = AP[h, 1]
        gr = a * QA[h]
        gl = a * SA[h]
        for k in range(B):
            c = CK[h, k][None]
            gr = gr + AP[h, k] * c
            gl = gl + WP[h, k] * c
        T1[pl.ds(h * M, M)] = gr
        SA[h] = gl

    mode_sums(0)
    relay(R2, E2, A0, (2, 3), True, 0)
    loop(H, mode_sums, 1)
    relay(R2, E2, A0, (2, 3), True, 1)
    loop(H, inside_back)

    @pl.when(me == n - 1)
    def _():
        for ref in (GF0, GF1, GF2):
            ref[pl.ds(rows, 8)] = jnp.zeros((8, H, 8, 128), f32)

    @pl.when(me < n - 1)
    def _():
        grad_copies[0].wait_recv()

    def back_filter(gf, i, slot):
        for h in range(H):

            def step(b):
                win = gf[pl.ds(b * B, B + HALO), h]
                store(slot, b, h, total(SW[i, h, j][None] * win[j : j + B] for j in range(KS)))

            loop(nb, step)


    def mixed(h, b, x):
        a = AP[h, 1]
        earlier = AP[h, B] * x + AB[h, b]
        SA[h] = SA[h] + x * PB[h, b]
        z = RA[h] * x
        for i in range(B):
            t = b * B + (B - 1 - i)
            g = G[t, h] + jnp.sum(z, axis=0)
            if i + 1 < B:
                z = a * z
            GF1[t, h] = g * F2[t, h]
            GF2[t, h] = g * F1[t, h]
        return earlier

    def reduce(src, dst, size):
        dst[...] = total(src[pl.ds(i * size, size)] for i in range(n))

    for h in range(H):
        arrived(A0.at[pl.ds(h * M, M)], 4 + h)
        if h == 0:
            scatter(T1, RR1, k3, (4, 6))
        lax.fori_loop(
            0, nb, lambda i, x: mixed(h, nb - 1 - i, x), A0[pl.ds(h * M, M)]
        )
        if h == H - 1:

            @pl.when(me > 0)
            def _():
                grad_copies[1].start()
                grad_copies[2].start()

        if h == 0:
            arrived(RR1A, 13)
            reduce(RR1A, SUM1A, k3)
            spread(SUM1A, AG1A, k3, (12, 14))
        mine = T2.at[h]
        mine[pl.ds(0, M)] = -RT[h] * SA[h]
        filter_sums(h, KX, GF1, mine, 16)
        filter_sums(h, VX, GF2, mine, 24)
        scatter(mine, RR2.at[h], k3, (6 + h, 8 + h))

    @pl.when(me < n - 1)
    def _():
        for copy in halo_copies:
            copy.wait_send()

    back_filter(GF0, 0, 1)

    arrived(RR2.at[0], 8)
    reduce(RR2.at[0], SUM2.at[0], k3)
    spread(SUM2.at[0], AG2.at[0], k3, (8, 10))

    arrived(RR1, 6)
    reduce(RR1, SUM1, k3)
    spread(SUM1, AG1, k3, (5, 7))

    for h in range(H):

        def late(b):
            at = pl.ds(b * B, B)
            gain = gainv[pl.ds(h * 8, 8), :][None]
            inv = jnp.stack([row(INVR, b * B + t) for t in range(B)])
            store(0, b, h, RS[at, h] * inv * gain)
            store(4, b, h, GS[at, h])

        loop(nb, late)

    for h in range(1, H):
        arrived(RR2.at[h], 8 + h)
        reduce(RR2.at[h], SUM2.at[h], k3)
        spread(SUM2.at[h], AG2.at[h], k3, (8 + h, 10 + h))

    @pl.when(me < n - 1)
    def _():
        grad_copies[1].wait_recv()
        grad_copies[2].wait_recv()

    back_filter(GF1, 1, 2)

    back_filter(GF2, 2, 3)

    def natural(src, at, count):
        return src[pl.ds(at, count)].reshape(count, 1024)

    arrived(AG1A, 14)
    arrived(AG1, 7)
    for h in range(H):
        cols = pl.ds(h * 1024, 1024)
        gr_o[:, cols] = natural(AG1, h * M, M)
        short_o[0, :, cols] = natural(AG1A, h * 8, 8)[0:KS]
        gskip_o[pl.ds(h * 8, 8), :] = AG1A[16 + h]
        ggain_o[pl.ds(h * 8, 8), :] = AG1A[18 + h]
    for h in range(H):
        cols = pl.ds(h * 1024, 1024)
        arrived(AG2.at[h], 10 + h)
        gl_o[:, cols] = natural(AG2.at[h], 0, M)
        short_o[1, :, cols] = natural(AG2.at[h], 16, 8)[0:KS]
        short_o[2, :, cols] = natural(AG2.at[h], 24, 8)[0:KS]

    for at, dst, size in (
        (0, R1, k1), (1, X0, k1), (2, R2, k1), (3, A0, k1), (4, RR1, k3), (5, AG1, k3), (11, RR1A, k3), (12, AG1A, k3),
        (6, RR2.at[0], k3), (7, RR2.at[1], k3), (8, AG2.at[0], k3), (9, AG2.at[1], k3),
    ):
        sent(dst, size, at)
    others = tpr.at[pl.ds(0, ntp - 1)]
    pltpu.make_async_copy(others, others, ssem.at[10]).wait()

    @pl.when(me > 0)
    def _():
        for copy in grad_copies:
            copy.wait_send()


def deliver(*refs):
    ins, outs, sem = refs[:10], refs[10:20], refs[20]
    copies = [pltpu.make_async_copy(s, d, sem.at[i]) for i, (s, d) in enumerate(zip(ins, outs))]
    for copy in copies:
        copy.start()
    for copy in copies:
        copy.wait()


def shards(
    n, ntp, residual, query_in, key_in, value_in, short_filter, residues, decay_rate, skip_gain,
    norm_gain, cotangent,
):
    rows, width = residual.shape
    H = width // 1024
    nb = rows // B
    tiles = H * M

    def V(*shape, dtype=f32):
        return pltpu.VMEM(shape, dtype)

    def tm(extra=0):
        return V(rows + extra, H, 8, 128)

    def tile(count):
        return V(count, 8, 128)

    k3 = 32 // n
    scratch = (
        [V(3, 8, width, dtype=bf16)]
        + [V(3, KS, width), V(M, width), V(M, width), V(H * 8, 128), V(H * 8, 128)]
        + [tm(8)] * 3 + [tm()] * 10 + [tm(8)] * 3
        + [V(H, B + 1, M, 8, 128)] * 2
        + [V(H, B + 1, 8, 128), V(H, M, 8, 128), V(H, M, 8, 128), V(3, H, 8, 8, 128), tile(tiles)]
        + [V(H, nb, M, 8, 128)] * 3
        + [tile(tiles)] * 8
        + [V(8, 128), tile(ntp), V(2, rows // 8, 8, 128), V(rows, 128), V(rows, 128)]
        + [V(H, M, 8, 128)] * 3
        + [V(H, B, 8, 128), V(8, 1024)]
        + [tile(32), tile(32), tile(k3), tile(32)] * 2
        + [V(H, 32, 8, 128), V(H, 32, 8, 128), V(H, k3, 8, 128), V(H, 32, 8, 128)]
        + [pltpu.SemaphoreType.DMA((c,)) for c in (10, 13, 15, 6, 6)]
    )
    big = jax.ShapeDtypeStruct((rows, width), bf16)
    vec = jax.ShapeDtypeStruct((H * 8, 128), f32)
    out_shape = (
        [big] * 5
        + [jax.ShapeDtypeStruct((3, KS, width), f32)]
        + [jax.ShapeDtypeStruct((M, width), f32)] * 2
        + [vec, vec]
    )
    anywhere = pl.BlockSpec(memory_space=pl.ANY)
    outs = pl.pallas_call(
        functools.partial(kernel, n, ntp, rows, width),
        out_shape=[V(*o.shape, dtype=o.dtype) for o in out_shape],
        in_specs=[anywhere] * 10,
        out_specs=[pl.BlockSpec(memory_space=pltpu.VMEM)] * 10,
        scratch_shapes=scratch,
        compiler_params=pltpu.CompilerParams(
            collective_id=0, has_side_effects=True, vmem_limit_bytes=52 << 20
        ),
    )(
        residual, query_in, key_in, value_in, short_filter, residues, decay_rate,
        skip_gain.reshape(H * 8, 128), norm_gain.reshape(H * 8, 128), cotangent,
    )
    outs = pl.pallas_call(
        deliver,
        out_shape=out_shape,
        in_specs=[anywhere] * 10,
        out_specs=[anywhere] * 10,
        scratch_shapes=[pltpu.SemaphoreType.DMA((10,))],
        compiler_params=pltpu.CompilerParams(vmem_limit_bytes=1 << 20),
    )(*outs)
    return (*outs[:8], outs[8].reshape(width), outs[9].reshape(width))


def solution(mesh):
    act, par, vec = P("ctx", "tp"), P(None, "tp"), P("tp")
    short = P(None, None, "tp")
    return jax.shard_map(
        functools.partial(shards, mesh.shape["ctx"], mesh.shape["tp"]),
        mesh=mesh,
        in_specs=(act, act, act, act, short, par, par, vec, vec, act),
        out_specs=(act, act, act, act, act, short, par, par, vec, vec),
        check_vma=False,
    )
```

```python
import functools

import jax
import jax.numpy as jnp
from jax import lax
from jax.experimental import pallas as pl
from jax.experimental.pallas import tpu as pltpu
from jax.sharding import PartitionSpec as P

f32 = jnp.float32
bf16 = jnp.bfloat16
MESH = pl.DeviceIdType.MESH
B = 16
M = 16
KS = 7
HALO = KS - 1


def loop(count, step, start=0):
    def lap(i, carry):
        step(i)
        return carry

    lax.fori_loop(start, count, lap, 0)


def total(terms):
    terms = list(terms)
    while len(terms) > 1:
        terms = [
            terms[i] + terms[i + 1] if i + 1 < len(terms) else terms[i]
            for i in range(0, len(terms), 2)
        ]
    return terms[0]


def kernel(
    n, ntp, rows, width,
    res_h, q_h, k_h, v_h, sf_h, r_h, lam_h, skip_h, gain_h, cot_h,
    normed_o, gres_o, gq_o, gk_o, gv_o, short_o, gr_o, gl_o, gskip_o, ggain_o,
    halo, sfv, rv, lv, skipv, gainv,
    QX, KX, VX, RS, CT, F0, F1, F2, U, Y, DZ, GS, G, GF0, GF1, GF2,
    AP, WP, KT, RT, LM, SW, AT, XB, PB, AB,
    S1, R1, E1, X0, S2, R2, E2, A0,
    sums, tpr, NS, INVR, CFR, RA, SA, QA, CK, SG,
    T1, RR1, SUM1, AG1, T1A, RR1A, SUM1A, AG1A, T2, RR2, SUM2, AG2,
    insem, ssem, rsem, hssem, hrsem,
):
    H = width // 1024
    nb = rows // B
    D = width * ntp
    me = lax.axis_index("ctx")
    mt = lax.axis_index("tp")
    tiles = H * M
    k1 = tiles // n
    k3 = 32 // n

    def peer(p):
        return (p, mt)

    nat = (normed_o, gq_o, gk_o, gv_o, gres_o)

    ins = [
        (lam_h, lv), (sf_h, sfv), (k_h, nat[2]), (v_h, nat[3]), (r_h, rv), (skip_h, skipv),
        (gain_h, gainv), (q_h, nat[1]), (res_h, nat[0]), (cot_h, nat[4]),
    ]
    in_copies = [pltpu.make_async_copy(s, d, insem.at[i]) for i, (s, d) in enumerate(ins)]
    for copy in in_copies:
        copy.start()

    barrier = pltpu.get_barrier_semaphore()

    for i in range(1, n):
        pl.semaphore_signal(
            barrier, inc=1, device_id=peer(lax.rem(me + i, n)), device_id_type=MESH
        )
    for i in range(1, ntp):
        pl.semaphore_signal(
            barrier, inc=1, device_id=(me, lax.rem(mt + i, ntp)), device_id_type=MESH
        )

    in_copies[0].wait()
    in_copies[1].wait()
    for h in range(H):
        cols = pl.ds(h * 1024, 1024)
        lam = lv[:, cols].reshape(M, 8, 128)
        AP[h, 1] = jnp.exp(-lam)
        AP[h, B] = jnp.exp(lam * (-float(B)))
        LM[h] = lam
        AT[pl.ds(h * M, M)] = jnp.exp(lam * (-float(rows)))
        for i in range(3):
            SG[0:8, :] = jnp.zeros((8, 1024), f32)
            SG[0:KS, :] = sfv[i, :, cols]
            SW[i, h] = SG[0:8, :].reshape(8, 8, 128)

    def to_tm(slot, dst, off):
        def step(i):
            v = nat[slot][pl.ds(pl.multiple_of(i * 16, 16), 16), :].astype(f32)
            dst[pl.ds(off + i * 16, 16)] = v.reshape(16, H, 8, 128)

        loop(rows // 16, step)

    in_copies[2].wait()
    to_tm(2, KX, 8)
    in_copies[3].wait()
    to_tm(3, VX, 8)

    pl.semaphore_wait(barrier, n - 1 + ntp - 1)

    def in_halo(i, src):
        return pltpu.make_async_remote_copy(
            src_ref=src.at[pl.ds(rows - 8, 8)], dst_ref=halo.at[i],
            send_sem=hssem.at[i], recv_sem=hrsem.at[i],
            device_id=peer(lax.rem(me + 1, n)), device_id_type=MESH,
        )

    halo_copies = [in_halo(0, q_h), in_halo(1, nat[2]), in_halo(2, nat[3])]

    @pl.when(me < n - 1)
    def _():
        for i in (1, 2, 0):
            halo_copies[i].start()

    def window(src, b, h):
        return src[pl.ds(b * 8 + 2, 14), h]

    def fir(win, i, h):
        return total(SW[i, h, j][None] * win[HALO - j : HALO - j + 8] for j in range(KS))

    def feature(h, b):
        at = pl.ds(b * 8, 8)
        f1 = fir(window(KX, b, h), 1, h)
        F1[at, h] = f1
        f2 = fir(window(VX, b, h), 2, h)
        F2[at, h] = f2
        U[at, h] = f1 * f2

    def gather(h, b):
        a = AP[h, 1]
        u = U[pl.ds(b * B, B), h]
        x = a * u[0][None] + u[1][None]
        for s in range(2, B):
            x = a * x + u[s][None]
        XB[h, b] = x
        return x

    def summary(h):
        def step(b, run):
            return AP[h, B] * run + gather(h, b)

        S1[pl.ds(h * M, M)] = lax.fori_loop(1, nb, step, jnp.zeros((M, 8, 128), f32))

    loop(rows // 8, functools.partial(feature, 0), 1)
    summary(0)
    for h in range(1, H):
        loop(rows // 8, functools.partial(feature, h), 1)

    def first_rows(i, dst):
        @pl.when(me > 0)
        def _():
            halo_copies[i].wait_recv()

        @pl.when(me == 0)
        def _():
            halo[i] = jnp.zeros(halo.shape[1:], bf16)

        dst[pl.ds(0, 8)] = halo[i].astype(f32).reshape(8, H, 8, 128)

    first_rows(1, KX)
    first_rows(2, VX)

    half = n // H

    def remote(src, dst, p, at):
        pltpu.make_async_remote_copy(
            src_ref=src, dst_ref=dst, send_sem=ssem.at[at[0]], recv_sem=rsem.at[at[1]],
            device_id=peer(p), device_id_type=MESH,
        ).start()

    def part(ref, p, size):
        return ref.at[pl.ds(p * size, size)]

    def scatter(src, dst, size, at):
        mine = part(dst, me, size)
        def step(i):
            p = lax.rem(me + lax.rem(i + n // 2 - 2, n - 1) + 1, n)
            remote(part(src, p, size), mine, p, at)

        loop(n, step, 1)
        pltpu.make_async_copy(part(src, me, size), mine, rsem.at[at[1]]).start()

    def scatter_half(src, dst, size, at, h):
        mine = part(dst, me, size)
        def step(i):
            p = h * half + lax.rem(me + i, half)
            remote(part(src, p, size), mine, p, at)

        loop(half, step, 1)
        first = me < half if h == 0 else me >= half
        other = me >= half if h == 0 else me < half

        @pl.when(first)
        def _():
            pltpu.make_async_copy(part(src, me, size), mine, rsem.at[at[1]]).start()

        @pl.when(other)
        def _():
            p = h * half + lax.rem(me, half)
            remote(part(src, p, size), mine, p, at)

    def spread(src, dst, size, at):
        mine = part(dst, me, size)
        loop(n, lambda i: remote(
            src, mine, lax.rem(me + lax.rem(i + n // 2 - 2, n - 1) + 1, n), at
        ), 1)
        pltpu.make_async_copy(src, mine, rsem.at[at[1]]).start()

    def arrived(dst, at):
        pltpu.make_async_copy(dst, dst, rsem.at[at]).wait()

    def sent(dst, size, at):
        all_but_one = dst.at[pl.ds(0, (n - 1) * size)]
        pltpu.make_async_copy(all_but_one, all_but_one, ssem.at[at]).wait()

    def scan(src, dst, backward):
        a = AT[pl.ds(me * k1, k1)]
        run = jnp.zeros((k1, 8, 128), f32)
        for i in range(n):
            d = n - 1 - i if backward else i
            at = pl.ds(d * k1, k1)
            dst[at] = run
            run = a * run + src[at]

    def relay(src, mid, dst, at, backward, h):
        @pl.when(me < half if h == 0 else me >= half)
        def _():
            arrived(src, at[1])
            scan(src, mid, backward)
            scatter(mid, dst, k1, (at[0] + 1, at[1] + 1 + h))

    for h in range(H):
        if h > 0:
            summary(h)
        feature(h, 0)
        S1[pl.ds(h * M, M)] = S1[pl.ds(h * M, M)] + gather(h, 0) * jnp.exp(
            LM[h] * (-float(rows - B))
        )
        scatter_half(S1, R1, k1, (0, 0), h)

    for i in (4, 5, 6):
        in_copies[i].wait()
    for h in range(H):
        r = rv[:, pl.ds(h * 1024, 1024)].reshape(M, 8, 128)
        RT[h] = r

        def powers(k):
            p = jnp.exp(LM[h] * (-k.astype(f32)))
            AP[h, k] = p
            WP[h, k] = p * k.astype(f32)
            KT[h, k] = jnp.sum(r * p, axis=0)

        loop(B + 1, powers)
        KT[h, 0] = KT[h, 0] + skipv[pl.ds(h * 8, 8), :]
        RA[h] = r * AP[h, 1]

    def inside(h):
        def step(b):
            u = [U[b * B + t, h] for t in range(B)]
            kt = [KT[h, k] for k in range(B)]
            for t in range(B):
                Y[b * B + t, h] = total(kt[k] * u[t - k] for k in range(t + 1))

        loop(nb, step)

    loop(H, inside)
    in_copies[7].wait()
    to_tm(1, QX, 8)
    first_rows(0, QX)
    relay(R1, E1, X0, (0, 0), False, 0)
    relay(R1, E1, X0, (0, 0), False, 1)

    def feature_q(h):
        def step(b):
            F0[pl.ds(b * 8, 8), h] = fir(window(QX, b, h), 0, h)

        loop(rows // 8, step)

    loop(H, feature_q)
    in_copies[8].wait()
    to_tm(0, RS, 0)
    in_copies[9].wait()
    gain_tm = gainv[...].reshape(1, H, 8, 128)

    def to_gain_term(i):
        v = nat[4][pl.ds(pl.multiple_of(i * 16, 16), 16), :].astype(f32)
        CT[pl.ds(i * 16, 16)] = v.reshape(16, H, 8, 128) * gain_tm

    loop(rows // 16, to_gain_term)

    def total_in_order(terms):
        out = terms[0]
        for term in terms[1:]:
            out = out + term
        return out

    def weighted(h):
        edge = (float(B) * AP[h, 1]) * AP[h, B]

        def step(b):
            u = U[pl.ds(b * B, B), h]
            PB[h, b] = total_in_order(
                [edge * XB[h, b]] + [WP[h, B - s] * u[s][None] for s in range(B)]
            )

        loop(nb, step)

    groups = rows // 8
    lane = lax.broadcasted_iota(jnp.int32, (8, 128), 1)

    def fold(parts):
        flat = jnp.stack(parts).reshape(8, 1024)
        return total(flat[:, i * 128 : (i + 1) * 128] for i in range(8))

    def forward(h, b, x):
        a = AP[h, 1]
        z = RA[h] * x
        later = AP[h, B] * x + XB[h, b]
        XB[h, b] = x
        squares, inner = [], []
        for i in range(B):
            t = b * B + i
            y = Y[t, h] + jnp.sum(z, axis=0)
            if i + 1 < B:
                z = a * z
            Y[t, h] = y
            s = RS[t, h] + F0[t, h] * y
            RS[t, h] = s
            squares.append(s * s)
            inner.append(CT[t, h] * s)
            if h > 0:
                squares[i] = squares[i] + G[t, 0]
                inner[i] = inner[i] + GS[t, 0]
            if h < H - 1:
                G[t, 0] = squares[i]
                GS[t, 0] = inner[i]
            if h == H - 1 and i % 8 == 7:
                NS[0, b * 2 + i // 8] = fold(squares[i - 7 : i + 1])
                NS[1, b * 2 + i // 8] = fold(inner[i - 7 : i + 1])
        return later

    for h in range(H):
        arrived(X0.at[pl.ds(h * M, M)], 1 + h)
        lax.fori_loop(0, nb, functools.partial(forward, h), X0[pl.ds(h * M, M)])
    gathered = jnp.zeros((8, 128), f32)
    for q in range(2):
        for g in range(groups):
            col = jnp.sum(NS[q, g], axis=1, keepdims=True)
            gathered = jnp.where(lane == q * groups + g, col, gathered)
    sums[...] = gathered
    for i in range(1, ntp):
        p = lax.rem(mt + i, ntp)
        pltpu.make_async_remote_copy(
            src_ref=sums, dst_ref=tpr.at[mt], send_sem=ssem.at[10], recv_sem=rsem.at[12],
            device_id=(me, p), device_id_type=MESH,
        ).start()
    pltpu.make_async_copy(sums, tpr.at[mt], rsem.at[12]).start()
    loop(H, weighted)
    arrived(tpr, 12)
    tot = total(tpr[i] for i in range(ntp))
    inner_sum = pltpu.roll(tot, 128 - groups, 1)
    valid = lane < groups
    inv_all = lax.rsqrt(jnp.where(valid, tot, 1.0) / D + 1e-5)
    coef_all = inv_all * inv_all * inv_all * jnp.where(valid, inner_sum, 0.0) / D

    for g in range(groups):
        at = pl.ds(g * 8, 8)
        INVR[at, :] = jnp.broadcast_to(inv_all[:, g : g + 1], (8, 128))
        CFR[at, :] = jnp.broadcast_to(coef_all[:, g : g + 1], (8, 128))

    def row(ref, t):
        return jnp.broadcast_to(ref[pl.ds(t, 1), :], (8, 128))

    def backward(h):
        a = AP[h, 1]

        def step(i, run):
            b = nb - 1 - i
            at = pl.ds(b * B, B)
            inv = jnp.stack([row(INVR, b * B + t) for t in range(B)])
            coef = jnp.stack([row(CFR, b * B + t) for t in range(B)])
            gs = inv * CT[at, h] - RS[at, h] * coef
            GS[at, h] = gs
            dz = gs * F0[at, h]
            DZ[at, h] = dz
            v = a * dz[B - 1][None] + dz[B - 2][None]
            for s in range(B - 3, -1, -1):
                v = a * v + dz[s][None]
            AB[h, b] = v
            return AP[h, B] * run + v

        S2[pl.ds(h * M, M)] = lax.fori_loop(0, nb, step, jnp.zeros((M, 8, 128), f32))

    for h in range(H):
        backward(h)
        scatter_half(S2, R2, k1, (2, 3), h)

    def store(slot, b, h, value):
        nat[slot][pl.ds(pl.multiple_of(b * 16, 16), 16), pl.ds(h * 1024, 1024)] = value.reshape(
            B, 1024
        ).astype(bf16)

    for h in range(H):

        def early(b, acc):
            at = pl.ds(b * B, B)
            GF0[at, h] = GS[at, h] * Y[at, h]
            inv = jnp.stack([row(INVR, b * B + t) for t in range(B)])
            return acc + jnp.sum(CT[at, h] * (RS[at, h] * inv), axis=0)

        acc = lax.fori_loop(0, nb, early, jnp.zeros((8, 128), f32))
        T1A[18 + h] = acc / gainv[pl.ds(h * 8, 8), :]

    def grad_halo(i, ref):
        return pltpu.make_async_remote_copy(
            src_ref=ref.at[pl.ds(0, HALO)], dst_ref=ref.at[pl.ds(rows, HALO)],
            send_sem=hssem.at[3 + i], recv_sem=hrsem.at[3 + i],
            device_id=peer(lax.rem(me + n - 1, n)), device_id_type=MESH,
        )

    grad_copies = [grad_halo(i, ref) for i, ref in enumerate((GF0, GF1, GF2))]

    @pl.when(me > 0)
    def _():
        grad_copies[0].start()

    def correlate(h):
        def step(b, acc):
            u = [U[b * B + t, h] for t in range(B)]
            dz = [DZ[b * B + t, h] for t in range(B)]
            return tuple(
                acc[k] + total(dz[t] * u[t - k] for t in range(k, B)) for k in range(B)
            )

        zero = jnp.zeros((8, 128), f32)
        out = lax.fori_loop(0, nb, step, (zero,) * B)
        for k in range(B):
            CK[h, k] = out[k]

    loop(H, correlate)

    def filter_sums(h, src, gf, dst, base):
        def step(b, acc):
            win = window(src, b, h)
            g = gf[pl.ds(b * 8, 8), h]
            return tuple(
                acc[j] + jnp.sum(g * win[HALO - j : HALO - j + 8], axis=0) for j in range(KS)
            )

        zero = jnp.zeros((8, 128), f32)
        out = lax.fori_loop(0, rows // 8, step, (zero,) * KS)
        for j in range(KS):
            dst[base + j] = out[j]
        dst[base + KS] = zero

    for h in range(H):
        filter_sums(h, QX, GF0, T1A, h * 8)
        T1A[16 + h] = CK[h, 0]
    T1A[pl.ds(18 + H, 14 - H)] = jnp.zeros((14 - H, 8, 128), f32)
    scatter(T1A, RR1A, k3, (11, 13))

    def inside_back(h):
        def step(b):
            dz = [DZ[b * B + t, h] for t in range(B)]
            kt = [KT[h, k] for k in range(B)]
            for s in range(B):
                G[b * B + s, h] = total(kt[k] * dz[s + k] for k in range(B - s))

        loop(nb, step)


    def mode_sums(h):
        def step(b):
            dz = DZ[pl.ds(b * B, B), h]
            x = XB[h, b]
            QA[h] = QA[h] + x * AB[h, b]
            q = total_in_order([WP[h, s] * dz[s][None] for s in range(1, B)])
            SA[h] = SA[h] + x * q

        QA[h] = jnp.zeros((M, 8, 128), f32)
        SA[h] = jnp.zeros((M, 8, 128), f32)
        loop(nb, step)
        a = AP[h, 1]
        gr = a * QA[h]
        gl = a * SA[h]
        for k in range(B):
            c = CK[h, k][None]
            gr = gr + AP[h, k] * c
            gl = gl + WP[h, k] * c
        T1[pl.ds(h * M, M)] = gr
        SA[h] = gl

    mode_sums(0)
    relay(R2, E2, A0, (2, 3), True, 0)
    loop(H, mode_sums, 1)
    relay(R2, E2, A0, (2, 3), True, 1)
    loop(H, inside_back)

    @pl.when(me == n - 1)
    def _():
        for ref in (GF0, GF1, GF2):
            ref[pl.ds(rows, 8)] = jnp.zeros((8, H, 8, 128), f32)

    @pl.when(me < n - 1)
    def _():
        grad_copies[0].wait_recv()

    def back_filter(gf, i, slot):
        for h in range(H):

            def step(b):
                win = gf[pl.ds(b * B, B + HALO), h]
                store(slot, b, h, total(SW[i, h, j][None] * win[j : j + B] for j in range(KS)))

            loop(nb, step)


    def mixed(h, b, x):
        a = AP[h, 1]
        earlier = AP[h, B] * x + AB[h, b]
        SA[h] = SA[h] + x * PB[h, b]
        z = RA[h] * x
        for i in range(B):
            t = b * B + (B - 1 - i)
            g = G[t, h] + jnp.sum(z, axis=0)
            if i + 1 < B:
                z = a * z
            GF1[t, h] = g * F2[t, h]
            GF2[t, h] = g * F1[t, h]
        return earlier

    def reduce(src, dst, size):
        dst[...] = total(src[pl.ds(i * size, size)] for i in range(n))

    for h in range(H):
        arrived(A0.at[pl.ds(h * M, M)], 4 + h)
        if h == 0:
            scatter(T1, RR1, k3, (4, 6))
        lax.fori_loop(
            0, nb, lambda i, x: mixed(h, nb - 1 - i, x), A0[pl.ds(h * M, M)]
        )
        if h == H - 1:

            @pl.when(me > 0)
            def _():
                grad_copies[1].start()
                grad_copies[2].start()

        if h == 0:
            arrived(RR1A, 13)
            reduce(RR1A, SUM1A, k3)
            spread(SUM1A, AG1A, k3, (12, 14))
        mine = T2.at[h]
        mine[pl.ds(0, M)] = -RT[h] * SA[h]
        filter_sums(h, KX, GF1, mine, 16)
        filter_sums(h, VX, GF2, mine, 24)
        scatter(mine, RR2.at[h], k3, (6 + h, 8 + h))

    @pl.when(me < n - 1)
    def _():
        for copy in halo_copies:
            copy.wait_send()

    back_filter(GF0, 0, 1)

    arrived(RR2.at[0], 8)
    reduce(RR2.at[0], SUM2.at[0], k3)
    spread(SUM2.at[0], AG2.at[0], k3, (8, 10))

    arrived(RR1, 6)
    reduce(RR1, SUM1, k3)
    spread(SUM1, AG1, k3, (5, 7))

    for h in range(H):

        def late(b):
            at = pl.ds(b * B, B)
            gain = gainv[pl.ds(h * 8, 8), :][None]
            inv = jnp.stack([row(INVR, b * B + t) for t in range(B)])
            store(0, b, h, RS[at, h] * inv * gain)
            store(4, b, h, GS[at, h])

        loop(nb, late)

    for h in range(1, H):
        arrived(RR2.at[h], 8 + h)
        reduce(RR2.at[h], SUM2.at[h], k3)
        spread(SUM2.at[h], AG2.at[h], k3, (8 + h, 10 + h))

    @pl.when(me < n - 1)
    def _():
        grad_copies[1].wait_recv()
        grad_copies[2].wait_recv()

    back_filter(GF1, 1, 2)

    back_filter(GF2, 2, 3)

    def natural(src, at, count):
        return src[pl.ds(at, count)].reshape(count, 1024)

    arrived(AG1A, 14)
    arrived(AG1, 7)
    for h in range(H):
        cols = pl.ds(h * 1024, 1024)
        gr_o[:, cols] = natural(AG1, h * M, M)
        short_o[0, :, cols] = natural(AG1A, h * 8, 8)[0:KS]
        gskip_o[pl.ds(h * 8, 8), :] = AG1A[16 + h]
        ggain_o[pl.ds(h * 8, 8), :] = AG1A[18 + h]
    for h in range(H):
        cols = pl.ds(h * 1024, 1024)
        arrived(AG2.at[h], 10 + h)
        gl_o[:, cols] = natural(AG2.at[h], 0, M)
        short_o[1, :, cols] = natural(AG2.at[h], 16, 8)[0:KS]
        short_o[2, :, cols] = natural(AG2.at[h], 24, 8)[0:KS]

    for at, dst, size in (
        (0, R1, k1), (1, X0, k1), (2, R2, k1), (3, A0, k1), (4, RR1, k3), (5, AG1, k3), (11, RR1A, k3), (12, AG1A, k3),
        (6, RR2.at[0], k3), (7, RR2.at[1], k3), (8, AG2.at[0], k3), (9, AG2.at[1], k3),
    ):
        sent(dst, size, at)
    others = tpr.at[pl.ds(0, ntp - 1)]
    pltpu.make_async_copy(others, others, ssem.at[10]).wait()

    @pl.when(me > 0)
    def _():
        for copy in grad_copies:
            copy.wait_send()


def deliver(*refs):
    ins, outs, sem = refs[:10], refs[10:20], refs[20]
    copies = [pltpu.make_async_copy(s, d, sem.at[i]) for i, (s, d) in enumerate(zip(ins, outs))]
    for copy in copies:
        copy.start()
    for copy in copies:
        copy.wait()


def shards(
    n, ntp, residual, query_in, key_in, value_in, short_filter, residues, decay_rate, skip_gain,
    norm_gain, cotangent,
):
    rows, width = residual.shape
    H = width // 1024
    nb = rows // B
    tiles = H * M

    def V(*shape, dtype=f32):
        return pltpu.VMEM(shape, dtype)

    def tm(extra=0):
        return V(rows + extra, H, 8, 128)

    def tile(count):
        return V(count, 8, 128)

    k3 = 32 // n
    scratch = (
        [V(3, 8, width, dtype=bf16)]
        + [V(3, KS, width), V(M, width), V(M, width), V(H * 8, 128), V(H * 8, 128)]
        + [tm(8)] * 3 + [tm()] * 10 + [tm(8)] * 3
        + [V(H, B + 1, M, 8, 128)] * 2
        + [V(H, B + 1, 8, 128), V(H, M, 8, 128), V(H, M, 8, 128), V(3, H, 8, 8, 128), tile(tiles)]
        + [V(H, nb, M, 8, 128)] * 3
        + [tile(tiles)] * 8
        + [V(8, 128), tile(ntp), V(2, rows // 8, 8, 128), V(rows, 128), V(rows, 128)]
        + [V(H, M, 8, 128)] * 3
        + [V(H, B, 8, 128), V(8, 1024)]
        + [tile(32), tile(32), tile(k3), tile(32)] * 2
        + [V(H, 32, 8, 128), V(H, 32, 8, 128), V(H, k3, 8, 128), V(H, 32, 8, 128)]
        + [pltpu.SemaphoreType.DMA((c,)) for c in (10, 13, 15, 6, 6)]
    )
    big = jax.ShapeDtypeStruct((rows, width), bf16)
    vec = jax.ShapeDtypeStruct((H * 8, 128), f32)
    out_shape = (
        [big] * 5
        + [jax.ShapeDtypeStruct((3, KS, width), f32)]
        + [jax.ShapeDtypeStruct((M, width), f32)] * 2
        + [vec, vec]
    )
    anywhere = pl.BlockSpec(memory_space=pl.ANY)
    outs = pl.pallas_call(
        functools.partial(kernel, n, ntp, rows, width),
        out_shape=[V(*o.shape, dtype=o.dtype) for o in out_shape],
        in_specs=[anywhere] * 10,
        out_specs=[pl.BlockSpec(memory_space=pltpu.VMEM)] * 10,
        scratch_shapes=scratch,
        compiler_params=pltpu.CompilerParams(
            collective_id=0, has_side_effects=True, vmem_limit_bytes=52 << 20
        ),
    )(
        residual, query_in, key_in, value_in, short_filter, residues, decay_rate,
        skip_gain.reshape(H * 8, 128), norm_gain.reshape(H * 8, 128), cotangent,
    )
    outs = pl.pallas_call(
        deliver,
        out_shape=out_shape,
        in_specs=[anywhere] * 10,
        out_specs=[anywhere] * 10,
        scratch_shapes=[pltpu.SemaphoreType.DMA((10,))],
        compiler_params=pltpu.CompilerParams(vmem_limit_bytes=1 << 20),
    )(*outs)
    return (*outs[:8], outs[8].reshape(width), outs[9].reshape(width))


def solution(mesh):
    act, par, vec = P("ctx", "tp"), P(None, "tp"), P("tp")
    short = P(None, None, "tp")
    return jax.shard_map(
        functools.partial(shards, mesh.shape["ctx"], mesh.shape["tp"]),
        mesh=mesh,
        in_specs=(act, act, act, act, short, par, par, vec, vec, act),
        out_specs=(act, act, act, act, act, short, par, par, vec, vec),
        check_vma=False,
    )
```
